32 devices in a mesh: scene: 4 (over y, x), row: 4 (over z), col: 2 (over core).
Axes of the slice: x: 2, y: 2, z: 4, core: 2. Of those that a mesh axis runs over, the one named last changes fastest.
Arguments:
- scenes: bfloat16 [4, 256, 128, 128], P('scene', 'row', 'col'), may hold values from -6 to 6
- cotangent: bfloat16 [4, 256, 128, 128], P('scene', 'row', 'col'), may hold values from -0.016479492 to 0.016479492
- params: float32 [294912], P(('scene', 'row', 'col')), may hold values from -0.1875 to 0.1875
- partials: float32 [32, 294912], P(('scene', 'row', 'col')), may hold values from -8 to 8
Outputs:
- sam_grad: float32 [294912], P(('scene', 'row', 'col'))
The draws below stay inside these ranges and needn't reach their ends.
All inputs are finite; a program needn't handle non-finite values.
Results may differ from the reference program's by a relative error of at most 0.0042.
Values may be sent and summed in bfloat16 or wider, within the bound.
A program may use at most 64 MiB of HBM per device.

```python
import jax
import jax.numpy as jnp
from jax import lax

C = 128
SCENES = 4
HEIGHT = 256
WIDTH = 128
DEVICES = 32


def with_spikes(result, stream_key, source, target, parts, factor):
    owner, partner = [(jnp.arange(result.shape[position]) // (result.shape[position] // parts)).reshape([-1 if axis == position else 1 for axis in range(result.ndim)]) for position in (source, target)]
    chosen = jax.random.permutation(stream_key, parts)[partner]
    strong = (owner == chosen) | (owner == (partner + parts // 2) % parts)
    return jnp.where(strong, factor * result, result)


def steps_of(rng, extent, cuts, smallest, top_value):
    loudness, own = 1.0, jax.random.fold_in(rng, 6)
    for position, shards_of in cuts:
        draws = jnp.exp(jax.random.uniform(jax.random.fold_in(own, position), (shards_of,), jnp.float32, smallest / len(cuts), top_value / len(cuts)))
        loudness = loudness * jnp.repeat(draws, extent[position] // shards_of).reshape([-1 if axis == position else 1 for axis in range(len(extent))])
    return loudness


def bell_draw(own_key, shape, scale, limit, shards=(), dtype=jnp.bfloat16):
    drawn = scale * jax.random.normal(own_key, shape, jnp.float32)
    if shards:
        drawn = drawn * steps_of(own_key, shape, shards, -0.22, 0.18)
    return jnp.clip(drawn, -limit, limit).astype(dtype)


def noise_with(own_key, dims, scale, bound, cuts, heavy, held_as=jnp.bfloat16):
    result = scale * jax.random.normal(own_key, dims, jnp.float32)
    if cuts:
        result = result * steps_of(own_key, dims, cuts, -0.22, 0.18)
    return jnp.clip(with_spikes(result, jax.random.fold_in(own_key, 3), *heavy), -bound, bound).astype(held_as)


def setup_inputs(seed: int = 0) -> dict:
    key_of = jax.random.split(jax.random.key(seed), 5)
    return {
        "scenes": bell_draw(key_of[0], (SCENES, HEIGHT, WIDTH, C), 1.0, 6.0, ((0, 4), (1, 4), (2, 2))),
        "cotangent": bell_draw(key_of[1], (SCENES, HEIGHT, WIDTH, C), ((SCENES * HEIGHT * WIDTH) ** -0.5), 0.016479492, ((0, 4), (1, 4), (2, 2))),
        "params": bell_draw(key_of[2], (18 * C * C,), (9 * C) ** -0.5, 0.1875, ((0, 32),), jnp.float32),
        "partials": noise_with(key_of[3], (DEVICES, 18 * C * C), 1.0, 8.0, ((0, 32),), (0, 1, 32, 2.75), jnp.float32),
    }


radius = 2.0
epsilon = 1e-06

def convolve(padded, kernel):
    return lax.conv_general_dilated(padded, kernel, (1, 1), 'VALID', dimension_numbers=('NHWC', 'HWIO', 'NHWC'), preferred_element_type=jnp.float32)

def border(field):
    return jnp.pad(field, ((0, 0), (1, 1), (1, 1), (0, 0)))

def kernel_grad(padded, errors):
    height = errors.shape[1]
    width = errors.shape[2]
    rows_out = []
    for row_off in range(3):
        cols_out = []
        for col_off in range(3):
            window = padded[:, row_off:row_off + height, col_off:col_off + width, :].astype(jnp.float32)
            cols_out.append(jnp.einsum('nhwc,nhwd->cd', window, errors.astype(jnp.float32)))
        rows_out.append(jnp.stack(cols_out))
    return jnp.stack(rows_out)

def reference(scenes, cotangent, params, partials):
    grads = lax.optimization_barrier(jnp.sum(partials, axis=0))
    factor = radius / (jnp.sqrt(jnp.sum(grads * grads)) + epsilon)
    perturbed = (params + factor * grads).astype(jnp.bfloat16)
    kernels = perturbed.reshape(2, 3, 3, scenes.shape[3], scenes.shape[3])
    kernel_one = kernels[0]
    kernel_two = kernels[1]
    flipped = jnp.transpose(kernel_two[::-1, ::-1], (0, 1, 3, 2))

    def one_scene(pair):
        inputs = pair[0][None]
        errors = pair[1][None]
        padded_in = border(inputs)
        pre = convolve(padded_in, kernel_one)
        hidden = jax.nn.silu(pre).astype(jnp.bfloat16)
        back = convolve(border(errors), flipped)
        squash = jax.nn.sigmoid(pre)
        delta = (back * squash * (1.0 + pre * (1.0 - squash))).astype(jnp.bfloat16)
        grad_one = kernel_grad(padded_in, delta)
        grad_two = kernel_grad(border(hidden), errors)
        return jnp.stack([grad_one, grad_two])
    per_scene = lax.map(one_scene, (scenes, cotangent))
    return lax.optimization_barrier(jnp.sum(per_scene, axis=0)).reshape(-1)
```

```python
import functools

import jax
import jax.numpy as jnp
from jax import lax
from jax.experimental import pallas as pl
from jax.experimental.pallas import tpu as pltpu
from jax.sharding import PartitionSpec as P

radius = 2.0
epsilon = 1e-06
AXES = ("scene", "row", "col")
MESH = pl.DeviceIdType.MESH
LANES = 128


class Place:
    def __init__(self, sizes):
        self.scenes, self.rows, self.cols = sizes
        self.pairs = self.cols // 2
        self.n = self.scenes * self.rows * self.pairs
        col = lax.axis_index("col")
        self.half = lax.rem(col, 2)
        self.me = (lax.axis_index("scene") * self.rows + lax.axis_index("row")) * self.pairs + col // 2

    def device(self, chip, half):
        return {
            "scene": chip // (self.rows * self.pairs),
            "row": lax.rem(chip // self.pairs, self.rows),
            "col": lax.rem(chip, self.pairs) * 2 + half,
        }

    def after(self, step):
        return lax.rem(self.me + step, self.n)

    def before(self, step):
        return lax.rem(self.me + self.n - step, self.n)


def loop(low, high, body):
    def wrapped(j, carry):
        body(j)
        return carry

    lax.fori_loop(low, high, wrapped, 0)


def wait_all(ref, sem):
    pltpu.make_async_copy(ref, ref, sem).wait()


def enter(place, everyone):
    barrier = pltpu.get_barrier_semaphore()

    def greet(j):
        chip = place.after(j)
        pl.semaphore_signal(barrier, inc=1, device_id=place.device(chip, place.half), device_id_type=MESH)
        if everyone:
            pl.semaphore_signal(barrier, inc=1, device_id=place.device(chip, 1 - place.half), device_id_type=MESH)

    pl.semaphore_signal(barrier, inc=1, device_id=place.device(place.me, 1 - place.half), device_id_type=MESH)
    loop(1, place.n, greet)
    pl.semaphore_wait(barrier, (2 * place.n - 1) if everyone else place.n)


def load_own(place, data, own, own_sem):
    def start(j):
        chip = place.after(j + 1)
        pltpu.make_async_copy(data.at[chip, place.half], own.at[chip], own_sem.at[j]).start()

    loop(0, place.n, start)


def scatter_sum(place, data, own, theirs, sums, landed, own_sem, swap_send, swap_recv, peer_send, peer_recv):
    n, me, half = place.n, place.me, place.half

    def swap(j):
        chip = place.after(j + 1)
        return pltpu.make_async_remote_copy(
            src_ref=data.at[chip, 1 - half],
            dst_ref=theirs.at[chip],
            send_sem=swap_send,
            recv_sem=swap_recv.at[j],
            device_id=place.device(me, 1 - half),
            device_id_type=MESH,
        )

    loop(0, n, lambda j: swap(j).start())

    def arrive(j):
        chip = place.after(j + 1)
        pltpu.make_async_copy(data.at[chip, half], own.at[chip], own_sem.at[j]).wait()
        swap(j).wait_recv()

    def pass_on(j):
        chip = place.after(j + 1)
        arrive(j)
        sums[j] = (own[chip] + theirs[chip]).astype(sums.dtype)
        pltpu.make_async_remote_copy(
            src_ref=sums.at[j],
            dst_ref=landed.at[j],
            send_sem=peer_send,
            recv_sem=peer_recv,
            device_id=place.device(chip, half),
            device_id_type=MESH,
        ).start()

    loop(0, n - 1, pass_on)
    arrive(n - 1)
    total = own[me] + theirs[me]
    wait_all(landed, peer_recv)
    total = lax.fori_loop(0, n - 1, lambda j, t: t + landed[j].astype(jnp.float32), total)
    wait_all(theirs, swap_send)
    wait_all(sums, peer_send)
    return total


def perturb_kernel(sizes, data, params, out, own, theirs, sums, landed, square, squares, mine,
                   own_sem, swap_send, swap_recv, peer_send, peer_recv,
                   sq_send, sq_recv, gather_send, gather_recv, relay_send, relay_recv):
    place = Place(sizes)
    n, me, half = place.n, place.me, place.half
    load_own(place, data, own, own_sem)
    enter(place, True)
    grads = scatter_sum(place, data, own, theirs, sums, landed, own_sem, swap_send, swap_recv, peer_send, peer_recv)

    local = jnp.sum(grads * grads)
    square[...] = jnp.full(square.shape, local, jnp.float32)

    def tell(chip, to_half, slot):
        pltpu.make_async_remote_copy(
            src_ref=square.at[0],
            dst_ref=squares.at[slot],
            send_sem=sq_send,
            recv_sem=sq_recv,
            device_id=place.device(chip, to_half),
            device_id_type=MESH,
        ).start()

    def tell_chip(j):
        chip = place.after(j)
        tell(chip, half, 2 * j - 1)
        tell(chip, 1 - half, 2 * j)

    tell(me, 1 - half, 0)
    loop(1, n, tell_chip)
    wait_all(squares, sq_recv)
    norm2 = square[0] + jnp.sum(squares[...], axis=0)
    factor = radius / (jnp.sqrt(norm2) + epsilon)
    mine[...] = (params[...] + factor * grads).astype(mine.dtype)
    wait_all(squares, sq_send)

    out[me, half] = mine[...]

    def relay(chip, j):
        return pltpu.make_async_remote_copy(
            src_ref=out.at[chip, half],
            dst_ref=out.at[chip, half],
            send_sem=relay_send,
            recv_sem=relay_recv,
            device_id=place.device(me, 1 - half),
            device_id_type=MESH,
        )

    def give(j):
        return pltpu.make_async_remote_copy(
            src_ref=mine,
            dst_ref=out.at[me, half],
            send_sem=gather_send,
            recv_sem=gather_recv.at[j],
            device_id=place.device(place.after(j + 1), half),
            device_id_type=MESH,
        )

    loop(0, n - 1, lambda j: give(j).start())
    pltpu.make_async_remote_copy(
        src_ref=mine,
        dst_ref=out.at[me, half],
        send_sem=relay_send,
        recv_sem=relay_recv,
        device_id=place.device(me, 1 - half),
        device_id_type=MESH,
    ).start()

    def pass_on(j):
        give(j).wait_recv()
        relay(place.before(j + 1), j).start()

    loop(0, n - 1, pass_on)
    wait_all(out.at[:, 0], relay_recv)
    wait_all(out.at[:, 0], relay_send)
    wait_all(landed, gather_send)


def scatter_kernel(sizes, data, out, own, theirs, sums, landed,
                   own_sem, swap_send, swap_recv, peer_send, peer_recv):
    place = Place(sizes)
    load_own(place, data, own, own_sem)
    enter(place, False)
    out[...] = scatter_sum(place, data, own, theirs, sums, landed, own_sem, swap_send, swap_recv, peer_send, peer_recv)


def sum_scratch(n, rows):
    dma = pltpu.SemaphoreType.DMA
    buffers = [
        pltpu.VMEM((n, rows, LANES), jnp.float32),
        pltpu.VMEM((n, rows, LANES), jnp.float32),
        pltpu.VMEM((n - 1, rows, LANES), jnp.bfloat16),
        pltpu.VMEM((n - 1, rows, LANES), jnp.bfloat16),
    ]
    return buffers, [dma((n,)), dma, dma((n,)), dma, dma]


def perturbed_params(sizes, local_part, share):
    n = sizes[0] * sizes[1] * sizes[2] // 2
    rows = share.size // LANES
    dma = pltpu.SemaphoreType.DMA
    buffers, sems = sum_scratch(n, rows)
    return pl.pallas_call(
        functools.partial(perturb_kernel, sizes),
        out_shape=jax.ShapeDtypeStruct((n, 2, rows, LANES), jnp.bfloat16),
        in_specs=[pl.BlockSpec(memory_space=pl.ANY), pl.BlockSpec(memory_space=pltpu.VMEM)],
        out_specs=pl.BlockSpec(memory_space=pltpu.VMEM),
        scratch_shapes=buffers
        + [
            pltpu.VMEM((1, 1, LANES), jnp.float32),
            pltpu.VMEM((2 * n - 1, 1, LANES), jnp.float32),
            pltpu.VMEM((rows, LANES), jnp.bfloat16),
        ]
        + sems
        + [dma, dma, dma, dma((n,)), dma, dma],
        compiler_params=pltpu.CompilerParams(collective_id=0, has_side_effects=True),
        cost_estimate=pl.CostEstimate(flops=1000000, bytes_accessed=60000000, transcendentals=0),
        name="perturb",
    )(local_part.reshape(n, 2, rows, LANES), share.reshape(rows, LANES))


def scattered_sum(sizes, local):
    n = sizes[0] * sizes[1] * sizes[2] // 2
    rows = local.size // (2 * n * LANES)
    buffers, sems = sum_scratch(n, rows)
    return pl.pallas_call(
        functools.partial(scatter_kernel, sizes),
        out_shape=jax.ShapeDtypeStruct((rows, LANES), jnp.float32),
        in_specs=[pl.BlockSpec(memory_space=pl.ANY)],
        out_specs=pl.BlockSpec(memory_space=pltpu.VMEM),
        scratch_shapes=buffers + sems,
        compiler_params=pltpu.CompilerParams(collective_id=1, has_side_effects=True),
        name="scatter_sum",
    )(local.reshape(n, 2, rows, LANES)).reshape(-1)


def with_halo(cells, sides, width):
    for axis, dim in sides:
        count = lax.axis_size(axis)
        ends = count - 1
        head = lax.slice_in_dim(cells, 0, width, axis=dim)
        tail = lax.slice_in_dim(cells, cells.shape[dim] - width, cells.shape[dim], axis=dim)
        cells = jnp.concatenate(
            [
                lax.ppermute(tail, axis, [(i, (i + 1) % count) for i in range(ends)]),
                cells,
                lax.ppermute(head, axis, [((i + 1) % count, i) for i in range(ends)]),
            ],
            axis=dim,
        )
    return cells


def convolve(padded, kernel):
    return lax.conv_general_dilated(
        padded,
        kernel,
        (1, 1),
        "VALID",
        dimension_numbers=("NHWC", "HWIO", "NHWC"),
        preferred_element_type=jnp.float32,
    )


def widened(field):
    return with_halo(field, (("row", 1), ("col", 2)), 1)


def kernel_grad(padded, errors):
    height = errors.shape[1]
    width = errors.shape[2]
    rows_out = []
    for row_off in range(3):
        cols_out = []
        for col_off in range(3):
            window = padded[:, row_off : row_off + height, col_off : col_off + width, :]
            cols_out.append(
                jnp.einsum("nhwc,nhwd->cd", window, errors, preferred_element_type=jnp.float32)
            )
        rows_out.append(jnp.stack(cols_out))
    return jnp.stack(rows_out)


def on_device(sizes, scenes, cotangent, params, partials):
    whole = perturbed_params(sizes, partials[0], params)
    channels = scenes.shape[3]
    kernels = whole.reshape(2, 3, 3, channels, channels)
    kernel_one = kernels[0]
    flipped = jnp.transpose(kernels[1][::-1, ::-1], (0, 1, 3, 2))
    padded_in = widened(scenes)
    pre = convolve(padded_in, kernel_one)
    hidden = jax.nn.silu(pre).astype(jnp.bfloat16)
    back = convolve(widened(cotangent), flipped)
    squash = jax.nn.sigmoid(pre)
    delta = (back * squash * (1.0 + pre * (1.0 - squash))).astype(jnp.bfloat16)
    grad_one = kernel_grad(padded_in, delta)
    grad_two = kernel_grad(widened(hidden), cotangent)
    local_grad = jnp.stack([grad_one, grad_two])
    return scattered_sum(sizes, local_grad)


def solution(mesh):
    sizes = tuple(mesh.shape[axis] for axis in AXES)
    return jax.shard_map(
        functools.partial(on_device, sizes),
        mesh=mesh,
        in_specs=(
            P("scene", "row", "col", None),
            P("scene", "row", "col", None),
            P(AXES),
            P(AXES, None),
        ),
        out_specs=P(AXES),
        check_vma=False,
    )
```

```python
import functools

import jax
import jax.numpy as jnp
from jax import lax
from jax.experimental import pallas as pl
from jax.experimental.pallas import tpu as pltpu
from jax.sharding import PartitionSpec as P

radius = 2.0
epsilon = 1e-06
AXES = ("scene", "row", "col")
MESH = pl.DeviceIdType.MESH
LANES = 128


class Place:
    def __init__(self, sizes):
        self.scenes, self.rows, self.cols = sizes
        self.pairs = self.cols // 2
        self.n = self.scenes * self.rows * self.pairs
        col = lax.axis_index("col")
        self.half = lax.rem(col, 2)
        self.me = (lax.axis_index("scene") * self.rows + lax.axis_index("row")) * self.pairs + col // 2

    def device(self, chip, half):
        return {
            "scene": chip // (self.rows * self.pairs),
            "row": lax.rem(chip // self.pairs, self.rows),
            "col": lax.rem(chip, self.pairs) * 2 + half,
        }

    def after(self, step):
        return lax.rem(self.me + step, self.n)

    def before(self, step):
        return lax.rem(self.me + self.n - step, self.n)


def loop(low, high, body):
    def wrapped(j, carry):
        body(j)
        return carry

    lax.fori_loop(low, high, wrapped, 0)


def wait_all(ref, sem):
    pltpu.make_async_copy(ref, ref, sem).wait()


def enter(place, everyone):
    barrier = pltpu.get_barrier_semaphore()

    def greet(j):
        chip = place.after(j)
        pl.semaphore_signal(barrier, inc=1, device_id=place.device(chip, place.half), device_id_type=MESH)
        if everyone:
            pl.semaphore_signal(barrier, inc=1, device_id=place.device(chip, 1 - place.half), device_id_type=MESH)

    pl.semaphore_signal(barrier, inc=1, device_id=place.device(place.me, 1 - place.half), device_id_type=MESH)
    loop(1, place.n, greet)
    pl.semaphore_wait(barrier, (2 * place.n - 1) if everyone else place.n)


def load_own(place, data, own, own_sem):
    def start(j):
        chip = place.after(j + 1)
        pltpu.make_async_copy(data.at[chip, place.half], own.at[chip], own_sem.at[j]).start()

    loop(0, place.n, start)


def scatter_sum(place, data, own, theirs, sums, landed, own_sem, swap_send, swap_recv, peer_send, peer_recv):
    n, me, half = place.n, place.me, place.half

    def swap(j):
        chip = place.after(j + 1)
        return pltpu.make_async_remote_copy(
            src_ref=data.at[chip, 1 - half],
            dst_ref=theirs.at[chip],
            send_sem=swap_send,
            recv_sem=swap_recv.at[j],
            device_id=place.device(me, 1 - half),
            device_id_type=MESH,
        )

    loop(0, n, lambda j: swap(j).start())

    def arrive(j):
        chip = place.after(j + 1)
        pltpu.make_async_copy(data.at[chip, half], own.at[chip], own_sem.at[j]).wait()
        swap(j).wait_recv()

    def pass_on(j):
        chip = place.after(j + 1)
        arrive(j)
        sums[j] = (own[chip] + theirs[chip]).astype(sums.dtype)
        pltpu.make_async_remote_copy(
            src_ref=sums.at[j],
            dst_ref=landed.at[j],
            send_sem=peer_send,
            recv_sem=peer_recv,
            device_id=place.device(chip, half),
            device_id_type=MESH,
        ).start()

    loop(0, n - 1, pass_on)
    arrive(n - 1)
    total = own[me] + theirs[me]
    wait_all(landed, peer_recv)
    total = lax.fori_loop(0, n - 1, lambda j, t: t + landed[j].astype(jnp.float32), total)
    wait_all(theirs, swap_send)
    wait_all(sums, peer_send)
    return total


AROUND = tuple((dr, dc) for dr in (-1, 0, 1) for dc in (-1, 0, 1) if dr or dc)


def edge_of(dr, dc):
    if dr:
        return 1 if dr < 0 else 0
    return 3 if dc < 0 else 2


def start_halo(sizes, edges, halo, halo_send, halo_recv):
    row, col = lax.axis_index("row"), lax.axis_index("col")
    for slot, (dr, dc) in enumerate(AROUND):
        pltpu.make_async_remote_copy(
            src_ref=edges.at[edge_of(dr, dc)],
            dst_ref=halo.at[slot],
            send_sem=halo_send,
            recv_sem=halo_recv,
            device_id={
                "scene": lax.axis_index("scene"),
                "row": lax.rem(row + sizes[1] - dr, sizes[1]),
                "col": lax.rem(col + sizes[2] - dc, sizes[2]),
            },
            device_id_type=MESH,
        ).start()


def perturb_kernel(sizes, data, params, edges, out, halo, own, theirs, sums, landed, square, squares, mine,
                   own_sem, swap_send, swap_recv, peer_send, peer_recv,
                   sq_send, sq_recv, gather_send, gather_recv, relay_send, relay_recv, halo_send, halo_recv):
    place = Place(sizes)
    n, me, half = place.n, place.me, place.half
    load_own(place, data, own, own_sem)
    enter(place, True)
    start_halo(sizes, edges, halo, halo_send, halo_recv)
    grads = scatter_sum(place, data, own, theirs, sums, landed, own_sem, swap_send, swap_recv, peer_send, peer_recv)

    local = jnp.sum(grads * grads)
    square[...] = jnp.full(square.shape, local, jnp.float32)

    def tell(chip, to_half, slot):
        pltpu.make_async_remote_copy(
            src_ref=square.at[0],
            dst_ref=squares.at[slot],
            send_sem=sq_send,
            recv_sem=sq_recv,
            device_id=place.device(chip, to_half),
            device_id_type=MESH,
        ).start()

    def tell_chip(j):
        chip = place.after(j)
        tell(chip, half, 2 * j - 1)
        tell(chip, 1 - half, 2 * j)

    tell(me, 1 - half, 0)
    loop(1, n, tell_chip)
    wait_all(squares, sq_recv)
    norm2 = square[0] + jnp.sum(squares[...], axis=0)
    factor = radius / (jnp.sqrt(norm2) + epsilon)
    mine[...] = (params[...] + factor * grads).astype(mine.dtype)
    wait_all(squares, sq_send)

    out[me, half] = mine[...]

    def relay(chip, j):
        return pltpu.make_async_remote_copy(
            src_ref=out.at[chip, half],
            dst_ref=out.at[chip, half],
            send_sem=relay_send,
            recv_sem=relay_recv,
            device_id=place.device(me, 1 - half),
            device_id_type=MESH,
        )

    def give(j):
        return pltpu.make_async_remote_copy(
            src_ref=mine,
            dst_ref=out.at[me, half],
            send_sem=gather_send,
            recv_sem=gather_recv.at[j],
            device_id=place.device(place.after(j + 1), half),
            device_id_type=MESH,
        )

    loop(0, n - 1, lambda j: give(j).start())
    pltpu.make_async_remote_copy(
        src_ref=mine,
        dst_ref=out.at[me, half],
        send_sem=relay_send,
        recv_sem=relay_recv,
        device_id=place.device(me, 1 - half),
        device_id_type=MESH,
    ).start()

    def pass_on(j):
        give(j).wait_recv()
        relay(place.before(j + 1), j).start()

    loop(0, n - 1, pass_on)
    wait_all(out.at[:, 0], relay_recv)
    wait_all(out.at[:, 0], relay_send)
    wait_all(landed, gather_send)
    wait_all(halo, halo_recv)
    wait_all(halo, halo_send)


def scatter_kernel(sizes, data, out, own, theirs, sums, landed,
                   own_sem, swap_send, swap_recv, peer_send, peer_recv):
    place = Place(sizes)
    load_own(place, data, own, own_sem)
    enter(place, False)
    out[...] = scatter_sum(place, data, own, theirs, sums, landed, own_sem, swap_send, swap_recv, peer_send, peer_recv)


def sum_scratch(n, rows):
    dma = pltpu.SemaphoreType.DMA
    buffers = [
        pltpu.VMEM((n, rows, LANES), jnp.float32),
        pltpu.VMEM((n, rows, LANES), jnp.float32),
        pltpu.VMEM((n - 1, rows, LANES), jnp.bfloat16),
        pltpu.VMEM((n - 1, rows, LANES), jnp.bfloat16),
    ]
    return buffers, [dma((n,)), dma, dma((n,)), dma, dma]


def perturbed_params(sizes, local_part, share, edges):
    n = sizes[0] * sizes[1] * sizes[2] // 2
    rows = share.size // LANES
    dma = pltpu.SemaphoreType.DMA
    buffers, sems = sum_scratch(n, rows)
    return pl.pallas_call(
        functools.partial(perturb_kernel, sizes),
        out_shape=(
            jax.ShapeDtypeStruct((n, 2, rows, LANES), jnp.bfloat16),
            jax.ShapeDtypeStruct((len(AROUND),) + edges.shape[1:], edges.dtype),
        ),
        in_specs=[pl.BlockSpec(memory_space=pl.ANY)] + [pl.BlockSpec(memory_space=pltpu.VMEM)] * 2,
        out_specs=(pl.BlockSpec(memory_space=pltpu.VMEM),) * 2,
        scratch_shapes=buffers
        + [
            pltpu.VMEM((1, 1, LANES), jnp.float32),
            pltpu.VMEM((2 * n - 1, 1, LANES), jnp.float32),
            pltpu.VMEM((rows, LANES), jnp.bfloat16),
        ]
        + sems
        + [dma, dma, dma, dma((n,)), dma, dma, dma, dma],
        compiler_params=pltpu.CompilerParams(collective_id=0, has_side_effects=True),
        cost_estimate=pl.CostEstimate(flops=1000000, bytes_accessed=60000000, transcendentals=0),
        name="perturb",
    )(local_part.reshape(n, 2, rows, LANES), share.reshape(rows, LANES), edges)


def scattered_sum(sizes, local):
    n = sizes[0] * sizes[1] * sizes[2] // 2
    rows = local.size // (2 * n * LANES)
    buffers, sems = sum_scratch(n, rows)
    return pl.pallas_call(
        functools.partial(scatter_kernel, sizes),
        out_shape=jax.ShapeDtypeStruct((rows, LANES), jnp.float32),
        in_specs=[pl.BlockSpec(memory_space=pl.ANY)],
        out_specs=pl.BlockSpec(memory_space=pltpu.VMEM),
        scratch_shapes=buffers + sems,
        compiler_params=pltpu.CompilerParams(collective_id=1, has_side_effects=True),
        name="scatter_sum",
    )(local.reshape(n, 2, rows, LANES)).reshape(-1)


def fill(sizes, which, cells, halo, cat, cols):
    height, width, channels = cells.shape
    row, col = lax.axis_index("row"), lax.axis_index("col")
    inside_row = {-1: row > 0, 0: row >= 0, 1: row < sizes[1] - 1}
    inside_col = {-1: col > 0, 0: col >= 0, 1: col < sizes[2] - 1}

    def arrived(dr, dc):
        inside = jnp.logical_and(inside_row[dr], inside_col[dc])
        block = halo[AROUND.index((dr, dc)), which].astype(jnp.float32)
        return jnp.where(inside, block, 0.0)

    position = lax.broadcasted_iota(jnp.int32, (width, channels), 0)

    def put(r, line, left, right):
        before = jnp.where(position == 0, left, pltpu.roll(line, 1, 0))
        behind = jnp.where(position == width - 1, right, pltpu.roll(line, width - 1, 0))
        cat[r, :, 0:channels] = before.astype(cat.dtype)
        cat[r, :, channels : 2 * channels] = line.astype(cat.dtype)
        cat[r, :, 2 * channels : 3 * channels] = behind.astype(cat.dtype)

    cols[0] = arrived(0, -1)
    cols[1] = arrived(0, 1)
    for dr, r in ((-1, 0), (1, height + 1)):
        put(r, arrived(dr, 0), arrived(dr, -1)[width - 1 : width], arrived(dr, 1)[0:1])

    def inner(r):
        put(r + 1, cells[r].astype(jnp.float32), cols[0, pl.ds(r, 1), :], cols[1, pl.ds(r, 1), :])

    loop(0, height, inner)


def windows(cat, start, rows):
    width, channels = cat.shape[1:]
    return jnp.concatenate(
        [cat[pl.ds(start + a, rows)].reshape(rows * width, channels) for a in range(3)], axis=1
    )


def over_cells(errors, field):
    return lax.dot_general(errors, field, (((0,), (0,)), ((), ())), preferred_element_type=jnp.float32)


def compute_kernel(sizes, block_rows, scenes, cotangent, halo, kernels, out, cat_in, cat_err, cols, flipped, acc_one, acc_two):
    height, width, channels = scenes.shape
    taps = 9
    fill(sizes, 0, scenes, halo, cat_in, cols)
    fill(sizes, 1, cotangent, halo, cat_err, cols)
    for t in range(taps):
        tap = kernels[1, taps - 1 - t].astype(jnp.float32)
        flipped[t * channels : (t + 1) * channels] = tap.T.astype(flipped.dtype)
    acc_one[...] = jnp.zeros_like(acc_one)
    acc_two[...] = jnp.zeros_like(acc_two)

    def step(i):
        start = i * block_rows
        fields = windows(cat_in, start, block_rows)
        errors = windows(cat_err, start, block_rows)
        pre = jnp.dot(fields, kernels[0].reshape(taps * channels, channels), preferred_element_type=jnp.float32)
        back = jnp.dot(errors, flipped[...], preferred_element_type=jnp.float32)
        squash = jax.nn.sigmoid(pre)
        hidden = (pre * squash).astype(jnp.bfloat16)
        delta = (back * squash * (1.0 + pre * (1.0 - squash))).astype(jnp.bfloat16)
        acc_one[...] += over_cells(delta, fields)
        acc_two[...] += over_cells(hidden, errors)

    loop(0, height // block_rows, step)
    for t in range(taps):
        out[t] = acc_one[:, t * channels : (t + 1) * channels].T
        u = taps - 1 - t
        out[taps + t] = acc_two[:, u * channels : (u + 1) * channels]


def local_grads(sizes, scenes, cotangent, halo, kernels):
    height, width, channels = scenes.shape
    block_rows = 8
    vmem = pl.BlockSpec(memory_space=pltpu.VMEM)
    cat = pltpu.VMEM((height + 2, width, 3 * channels), jnp.bfloat16)
    acc = pltpu.VMEM((channels, 9 * channels), jnp.float32)
    return pl.pallas_call(
        functools.partial(compute_kernel, sizes, block_rows),
        out_shape=jax.ShapeDtypeStruct((18, channels, channels), jnp.float32),
        in_specs=[vmem] * 4,
        out_specs=vmem,
        scratch_shapes=[
            cat,
            cat,
            pltpu.VMEM((2, height, channels), jnp.float32),
            pltpu.VMEM((9 * channels, channels), jnp.bfloat16),
            acc,
            acc,
        ],
        compiler_params=pltpu.CompilerParams(vmem_limit_bytes=56 * 2**20),
        name="local_grads",
    )(scenes, cotangent, halo, kernels)


def on_device(sizes, scenes, cotangent, params, partials):
    scenes, cotangent = scenes[0], cotangent[0]
    channels = scenes.shape[2]
    edges = jnp.stack(
        [jnp.stack([x[0], x[-1], x[:, 0], x[:, -1]]) for x in (scenes, cotangent)], axis=1
    )
    whole, halo = perturbed_params(sizes, partials[0], params, edges)
    kernels = whole.reshape(2, 9, channels, channels)
    return scattered_sum(sizes, local_grads(sizes, scenes, cotangent, halo, kernels))


def solution(mesh):
    sizes = tuple(mesh.shape[axis] for axis in AXES)
    return jax.shard_map(
        functools.partial(on_device, sizes),
        mesh=mesh,
        in_specs=(
            P("scene", "row", "col", None),
            P("scene", "row", "col", None),
            P(AXES),
            P(AXES, None),
        ),
        out_specs=P(AXES),
        check_vma=False,
    )
```

```python
import functools

import jax
import jax.numpy as jnp
from jax import lax
from jax.experimental import pallas as pl
from jax.experimental.pallas import tpu as pltpu
from jax.sharding import PartitionSpec as P

radius = 2.0
epsilon = 1e-06
AXES = ("scene", "row", "col")
MESH = pl.DeviceIdType.MESH
LANES = 128


class Place:
    def __init__(self, sizes):
        self.scenes, self.rows, self.cols = sizes
        self.pairs = self.cols // 2
        self.n = self.scenes * self.rows * self.pairs
        col = lax.axis_index("col")
        self.half = lax.rem(col, 2)
        self.me = (lax.axis_index("scene") * self.rows + lax.axis_index("row")) * self.pairs + col // 2

    def device(self, chip, half):
        return {
            "scene": chip // (self.rows * self.pairs),
            "row": lax.rem(chip // self.pairs, self.rows),
            "col": lax.rem(chip, self.pairs) * 2 + half,
        }

    def after(self, step):
        return lax.rem(self.me + step, self.n)

    def before(self, step):
        return lax.rem(self.me + self.n - step, self.n)


def loop(low, high, body):
    def wrapped(j, carry):
        body(j)
        return carry

    lax.fori_loop(low, high, wrapped, 0)


def wait_all(ref, sem):
    pltpu.make_async_copy(ref, ref, sem).wait()


def greet_all(place):
    barrier = pltpu.get_barrier_semaphore()

    def greet(j):
        chip = place.after(j)
        pl.semaphore_signal(barrier, inc=1, device_id=place.device(chip, place.half), device_id_type=MESH)
        pl.semaphore_signal(barrier, inc=1, device_id=place.device(chip, 1 - place.half), device_id_type=MESH)

    pl.semaphore_signal(barrier, inc=1, device_id=place.device(place.me, 1 - place.half), device_id_type=MESH)
    loop(1, place.n, greet)
    return barrier


def scatter_sum(place, data, own, theirs, sums, landed, swap_send, swap_recv, peer_send, peer_recv):
    n, me, half = place.n, place.me, place.half

    def swap(j):
        chip = place.after(j + 1)
        return pltpu.make_async_remote_copy(
            src_ref=data.at[chip, 1 - half],
            dst_ref=theirs.at[chip],
            send_sem=swap_send,
            recv_sem=swap_recv.at[j],
            device_id=place.device(me, 1 - half),
            device_id_type=MESH,
        )

    loop(0, n, lambda j: swap(j).start())

    def both(j):
        chip = place.after(j + 1)
        mine = own(j, chip)
        swap(j).wait_recv()
        return mine + theirs[chip]

    def pass_on(j):
        sums[j] = both(j).astype(sums.dtype)
        pltpu.make_async_remote_copy(
            src_ref=sums.at[j],
            dst_ref=landed.at[j],
            send_sem=peer_send,
            recv_sem=peer_recv,
            device_id=place.device(place.after(j + 1), half),
            device_id_type=MESH,
        ).start()

    loop(0, n - 1, pass_on)
    total = both(n - 1)
    wait_all(landed, peer_recv)
    total = lax.fori_loop(0, n - 1, lambda j, t: t + landed[j].astype(jnp.float32), total)
    wait_all(theirs, swap_send)
    wait_all(sums, peer_send)
    return total


AROUND = tuple((dr, dc) for dr in (-1, 0, 1) for dc in (-1, 0, 1) if dr or dc)


def edge_of(dr, dc):
    if dr:
        return 1 if dr < 0 else 0
    return 3 if dc < 0 else 2


def start_halo(sizes, edges, halo, halo_send, halo_recv):
    row, col = lax.axis_index("row"), lax.axis_index("col")
    for slot, (dr, dc) in enumerate(AROUND):
        pltpu.make_async_remote_copy(
            src_ref=edges.at[edge_of(dr, dc)],
            dst_ref=halo.at[slot],
            send_sem=halo_send,
            recv_sem=halo_recv,
            device_id={
                "scene": lax.axis_index("scene"),
                "row": lax.rem(row + sizes[1] - dr, sizes[1]),
                "col": lax.rem(col + sizes[2] - dc, sizes[2]),
            },
            device_id_type=MESH,
        ).start()


def fill(sizes, which, cells, halo, cat, cols):
    height, width, channels = cells.shape
    row, col = lax.axis_index("row"), lax.axis_index("col")
    inside_row = {-1: row > 0, 0: row >= 0, 1: row < sizes[1] - 1}
    inside_col = {-1: col > 0, 0: col >= 0, 1: col < sizes[2] - 1}

    def arrived(dr, dc):
        inside = jnp.logical_and(inside_row[dr], inside_col[dc])
        block = halo[AROUND.index((dr, dc)), which].astype(jnp.float32)
        return jnp.where(inside, block, 0.0)

    position = lax.broadcasted_iota(jnp.int32, (width, channels), 0)

    def put(r, line, left, right):
        before = jnp.where(position == 0, left, pltpu.roll(line, 1, 0))
        behind = jnp.where(position == width - 1, right, pltpu.roll(line, width - 1, 0))
        cat[r, :, 0:channels] = before.astype(cat.dtype)
        cat[r, :, channels : 2 * channels] = line.astype(cat.dtype)
        cat[r, :, 2 * channels : 3 * channels] = behind.astype(cat.dtype)

    cols[0] = arrived(0, -1)
    cols[1] = arrived(0, 1)
    for dr, r in ((-1, 0), (1, height + 1)):
        put(r, arrived(dr, 0), arrived(dr, -1)[width - 1 : width], arrived(dr, 1)[0:1])

    def inner(r):
        put(r + 1, cells[r].astype(jnp.float32), cols[0, pl.ds(r, 1), :], cols[1, pl.ds(r, 1), :])

    loop(0, height, inner)


def windows(cat, start, rows):
    width, channels = cat.shape[1:]
    return jnp.concatenate(
        [cat[pl.ds(start + a, rows)].reshape(rows * width, channels) for a in range(3)], axis=1
    )


def over_cells(errors, field):
    return lax.dot_general(errors, field, (((0,), (0,)), ((), ())), preferred_element_type=jnp.float32)


def kernel(sizes, block_rows, data, params, scenes_hbm, cotangent_hbm, out,
           scenes, cotangent, edges, halo, cat_in, cat_err, cols, flat, ones, flipped, acc_one, acc_two, whole, local,
           own, theirs, sums, landed, square, squares, mine, theirs_b, sums_b, landed_b,
           load_sem, own_sem, swap_send, swap_recv, peer_send, peer_recv,
           sq_send, sq_recv, gather_send, gather_recv, relay_send, relay_recv, halo_send, halo_recv,
           swap_send_b, swap_recv_b, peer_send_b, peer_recv_b):
    place = Place(sizes)
    n, me, half = place.n, place.me, place.half
    height, width, channels = scenes.shape
    rows = params.shape[0]
    taps = 9

    loads = [
        pltpu.make_async_copy(scenes_hbm, scenes, load_sem.at[0]),
        pltpu.make_async_copy(cotangent_hbm, cotangent, load_sem.at[1]),
    ]
    for load in loads:
        load.start()

    def load_own(j):
        chip = place.after(j + 1)
        return pltpu.make_async_copy(data.at[chip, half], own.at[chip], own_sem.at[j])

    loop(0, n, lambda j: load_own(j).start())
    barrier = greet_all(place)
    for which, (load, cells) in enumerate(zip(loads, (scenes, cotangent))):
        load.wait()
        edges[0, which] = cells[0]
        edges[1, which] = cells[height - 1]
        edges[2, which] = cells[:, 0:16, :].astype(jnp.float32)[:, 0, :].astype(edges.dtype)
        edges[3, which] = cells[:, width - 16 : width, :].astype(jnp.float32)[:, 15, :].astype(edges.dtype)
    pl.semaphore_wait(barrier, 2 * n - 1)

    def loaded(j, chip):
        load_own(j).wait()
        return own[chip]

    start_halo(sizes, edges, halo, halo_send, halo_recv)
    grads = scatter_sum(place, data, loaded, theirs, sums, landed, swap_send, swap_recv, peer_send, peer_recv)

    square[...] = jnp.full(square.shape, jnp.sum(grads * grads), jnp.float32)

    def tell(chip, to_half, slot):
        pltpu.make_async_remote_copy(
            src_ref=square.at[0],
            dst_ref=squares.at[slot],
            send_sem=sq_send,
            recv_sem=sq_recv,
            device_id=place.device(chip, to_half),
            device_id_type=MESH,
        ).start()

    def tell_chip(j):
        chip = place.after(j)
        tell(chip, half, 2 * j - 1)
        tell(chip, 1 - half, 2 * j)

    loop(1, n, tell_chip)
    tell(me, 1 - half, 0)

    wait_all(halo, halo_recv)
    fill(sizes, 0, scenes, halo, cat_in, cols)
    fill(sizes, 1, cotangent, halo, cat_err, cols)

    wait_all(squares, sq_recv)
    norm2 = square[0] + jnp.sum(squares[...], axis=0)
    factor = radius / (jnp.sqrt(norm2) + epsilon)
    mine[...] = (params[...] + factor * grads).astype(mine.dtype)
    whole[me, half] = mine[...]

    def relay(src, chip):
        return pltpu.make_async_remote_copy(
            src_ref=src,
            dst_ref=whole.at[chip, half],
            send_sem=relay_send,
            recv_sem=relay_recv,
            device_id=place.device(me, 1 - half),
            device_id_type=MESH,
        )

    def give(j):
        return pltpu.make_async_remote_copy(
            src_ref=mine,
            dst_ref=whole.at[me, half],
            send_sem=gather_send,
            recv_sem=gather_recv.at[j],
            device_id=place.device(place.after(j + 1), half),
            device_id_type=MESH,
        )

    loop(0, n - 1, lambda j: give(j).start())
    relay(mine, me).start()

    def hand_over(j):
        chip = place.before(j + 1)
        give(j).wait_recv()
        relay(whole.at[chip, half], chip).start()

    loop(0, n - 1, hand_over)
    wait_all(whole.at[:, 0], relay_recv)
    wait_all(whole.at[:, 0], relay_send)
    wait_all(landed, gather_send)
    wait_all(squares, sq_send)
    wait_all(halo, halo_send)

    def spread(c):
        flat[pl.ds(c * rows, rows), :] = whole[c // 2, lax.rem(c, 2)].astype(jnp.float32)

    loop(0, 2 * n, spread)
    ones[...] = flat[0 : taps * channels].astype(ones.dtype)
    for t in range(taps):
        first = (2 * taps - 1 - t) * channels
        flipped[t * channels : (t + 1) * channels] = flat[first : first + channels].T.astype(flipped.dtype)
    acc_one[...] = jnp.zeros_like(acc_one)
    acc_two[...] = jnp.zeros_like(acc_two)

    def step(i):
        start = i * block_rows
        fields = windows(cat_in, start, block_rows)
        errors = windows(cat_err, start, block_rows)
        pre = jnp.dot(fields, ones[...], preferred_element_type=jnp.float32)
        back = jnp.dot(errors, flipped[...], preferred_element_type=jnp.float32)
        squash = jax.nn.sigmoid(pre)
        hidden = (pre * squash).astype(jnp.bfloat16)
        delta = (back * squash * (1.0 + pre * (1.0 - squash))).astype(jnp.bfloat16)
        acc_one[...] += over_cells(delta, fields)
        acc_two[...] += over_cells(hidden, errors)

    loop(0, height // block_rows, step)
    for t in range(taps):
        flat[t * channels : (t + 1) * channels] = acc_one[:, t * channels : (t + 1) * channels].T
        u = taps - 1 - t
        flat[(taps + t) * channels : (taps + t + 1) * channels] = acc_two[:, u * channels : (u + 1) * channels]

    def collect(c):
        local[c // 2, lax.rem(c, 2)] = flat[pl.ds(c * rows, rows), :]

    loop(0, 2 * n, collect)
    out[...] = scatter_sum(
        place, local, lambda j, chip: local[chip, half], theirs_b, sums_b, landed_b,
        swap_send_b, swap_recv_b, peer_send_b, peer_recv_b,
    )


def on_device(sizes, scenes, cotangent, params, partials):
    scenes, cotangent = scenes[0], cotangent[0]
    height, width, channels = scenes.shape
    n = sizes[0] * sizes[1] * sizes[2] // 2
    rows = params.size // LANES
    dma = pltpu.SemaphoreType.DMA
    half_type, full = jnp.bfloat16, jnp.float32
    anywhere, vmem = pl.BlockSpec(memory_space=pl.ANY), pl.BlockSpec(memory_space=pltpu.VMEM)
    cat = pltpu.VMEM((height + 2, width, 3 * channels), half_type)
    tall = pltpu.VMEM((9 * channels, channels), half_type)
    acc = pltpu.VMEM((channels, 9 * channels), full)
    chunks = [
        pltpu.VMEM((n, rows, LANES), full),
        pltpu.VMEM((n - 1, rows, LANES), half_type),
        pltpu.VMEM((n - 1, rows, LANES), half_type),
    ]
    scratch = [
        pltpu.VMEM(scenes.shape, half_type),
        pltpu.VMEM(scenes.shape, half_type),
        pltpu.VMEM((4, 2, width, channels), half_type),
        pltpu.VMEM((len(AROUND), 2, width, channels), half_type),
        cat,
        cat,
        pltpu.VMEM((2, height, channels), full),
        pltpu.VMEM((18 * channels, channels), full),
        tall,
        tall,
        acc,
        acc,
        pltpu.VMEM((n, 2, rows, LANES), half_type),
        pltpu.VMEM((n, 2, rows, LANES), full),
        pltpu.VMEM((n, rows, LANES), full),
        *chunks,
        pltpu.VMEM((1, 1, LANES), full),
        pltpu.VMEM((2 * n - 1, 1, LANES), full),
        pltpu.VMEM((rows, LANES), half_type),
        *chunks,
        dma((2,)), dma((n,)), dma, dma((n,)), dma, dma,
        dma, dma, dma, dma((n,)), dma, dma, dma, dma,
        dma, dma((n,)), dma, dma,
    ]
    grads = pl.pallas_call(
        functools.partial(kernel, sizes, 8),
        out_shape=jax.ShapeDtypeStruct((rows, LANES), full),
        in_specs=[anywhere, vmem, anywhere, anywhere],
        out_specs=vmem,
        scratch_shapes=scratch,
        compiler_params=pltpu.CompilerParams(
            collective_id=0, has_side_effects=True, vmem_limit_bytes=56 * 2**20
        ),
        name="sam_grad",
    )(partials[0].reshape(n, 2, rows, LANES), params.reshape(rows, LANES), scenes, cotangent)
    return grads.reshape(-1)


def solution(mesh):
    sizes = tuple(mesh.shape[axis] for axis in AXES)
    return jax.shard_map(
        functools.partial(on_device, sizes),
        mesh=mesh,
        in_specs=(
            P("scene", "row", "col", None),
            P("scene", "row", "col", None),
            P(AXES),
            P(AXES, None),
        ),
        out_specs=P(AXES),
        check_vma=False,
    )
```

```python
import functools

import jax
import jax.numpy as jnp
from jax import lax
from jax.experimental import pallas as pl
from jax.experimental.pallas import tpu as pltpu
from jax.sharding import PartitionSpec as P

radius = 2.0
epsilon = 1e-06
AXES = ("scene", "row", "col")
MESH = pl.DeviceIdType.MESH
LANES = 128


class Place:
    def __init__(self, sizes):
        self.scenes, self.rows, self.cols = sizes
        self.pairs = self.cols // 2
        self.n = self.scenes * self.rows * self.pairs
        col = lax.axis_index("col")
        self.half = lax.rem(col, 2)
        self.m = self.scenes * self.pairs
        self.row = lax.axis_index("row")
        self.plane = lax.axis_index("scene") * self.pairs + col // 2
        self.me = self.chip(self.plane, self.row)

    def chip(self, plane, row):
        return (plane // self.pairs * self.rows + row) * self.pairs + lax.rem(plane, self.pairs)

    def plane_after(self, u):
        return lax.rem(self.plane + 1 + u, self.m)

    def row_after(self, t):
        return lax.rem(self.row + 1 + t, self.rows)

    def order(self, j):
        return self.chip(self.plane_after(lax.rem(j, self.m)), self.row_after(j // self.m))

    def device(self, chip, half):
        return {
            "scene": chip // (self.rows * self.pairs),
            "row": lax.rem(chip // self.pairs, self.rows),
            "col": lax.rem(chip, self.pairs) * 2 + half,
        }

    def after(self, step):
        return lax.rem(self.me + step, self.n)


def loop(low, high, body):
    def wrapped(j, carry):
        body(j)
        return carry

    lax.fori_loop(low, high, wrapped, 0)


def wait_all(ref, sem):
    pltpu.make_async_copy(ref, ref, sem).wait()


def greet_all(place):
    barrier = pltpu.get_barrier_semaphore()

    def greet(j):
        chip = place.after(j)
        pl.semaphore_signal(barrier, inc=1, device_id=place.device(chip, place.half), device_id_type=MESH)
        pl.semaphore_signal(barrier, inc=1, device_id=place.device(chip, 1 - place.half), device_id_type=MESH)

    pl.semaphore_signal(barrier, inc=1, device_id=place.device(place.me, 1 - place.half), device_id_type=MESH)
    loop(1, place.n, greet)
    return barrier


def scatter_sum(place, data, own, theirs, sums, landed, kept, reached,
                swap_send, swap_recv, plane_send, plane_recv, row_send, row_recv):
    n, m, rows, me, half = place.n, place.m, place.rows, place.me, place.half
    full = jnp.float32

    def swap(j):
        chip = place.order(j)
        return pltpu.make_async_remote_copy(
            src_ref=data.at[chip, 1 - half],
            dst_ref=theirs.at[chip],
            send_sem=swap_send,
            recv_sem=swap_recv.at[j],
            device_id=place.device(me, 1 - half),
            device_id_type=MESH,
        )

    loop(0, n, lambda j: swap(j).start())

    def both(j):
        chip = place.order(j)
        mine = own(j, chip)
        swap(j).wait_recv()
        return mine + theirs[chip]

    def across_plane(t):
        def pass_on(u):
            slot = t * (m - 1) + u
            sums[slot] = both(t * m + u).astype(sums.dtype)
            pltpu.make_async_remote_copy(
                src_ref=sums.at[slot],
                dst_ref=landed.at[t, u],
                send_sem=plane_send,
                recv_sem=plane_recv.at[t],
                device_id=place.device(place.chip(place.plane_after(u), place.row), half),
                device_id_type=MESH,
            ).start()

        loop(0, m - 1, pass_on)
        kept[t] = both(t * m + m - 1)

    loop(0, rows, across_plane)

    def plane_total(t):
        wait_all(landed.at[t], plane_recv.at[t])
        return lax.fori_loop(0, m - 1, lambda u, sofar: sofar + landed[t, u].astype(full), kept[t])

    def along_rows(t):
        kept[t] = plane_total(t)
        pltpu.make_async_remote_copy(
            src_ref=kept.at[t],
            dst_ref=reached.at[t],
            send_sem=row_send,
            recv_sem=row_recv,
            device_id=place.device(place.chip(place.plane, place.row_after(t)), half),
            device_id_type=MESH,
        ).start()

    loop(0, rows - 1, along_rows)
    total = plane_total(rows - 1)
    wait_all(reached, row_recv)
    total = lax.fori_loop(0, rows - 1, lambda t, sofar: sofar + reached[t], total)
    wait_all(theirs, swap_send)
    wait_all(sums, plane_send)
    wait_all(reached, row_send)
    return total


AROUND = tuple((dr, dc) for dr in (-1, 0, 1) for dc in (-1, 0, 1) if dr or dc)


def edge_of(dr, dc):
    if dr:
        return 1 if dr < 0 else 0
    return 3 if dc < 0 else 2


def start_halo(sizes, edges, halo, halo_send, halo_recv):
    row, col = lax.axis_index("row"), lax.axis_index("col")
    for slot, (dr, dc) in enumerate(AROUND):
        pltpu.make_async_remote_copy(
            src_ref=edges.at[edge_of(dr, dc)],
            dst_ref=halo.at[slot],
            send_sem=halo_send,
            recv_sem=halo_recv,
            device_id={
                "scene": lax.axis_index("scene"),
                "row": lax.rem(row + sizes[1] - dr, sizes[1]),
                "col": lax.rem(col + sizes[2] - dc, sizes[2]),
            },
            device_id_type=MESH,
        ).start()


def fill(sizes, which, cells, halo, cat, cols):
    height, width, channels = cells.shape
    row, col = lax.axis_index("row"), lax.axis_index("col")
    inside_row = {-1: row > 0, 0: row >= 0, 1: row < sizes[1] - 1}
    inside_col = {-1: col > 0, 0: col >= 0, 1: col < sizes[2] - 1}

    def arrived(dr, dc):
        inside = jnp.logical_and(inside_row[dr], inside_col[dc])
        block = halo[AROUND.index((dr, dc)), which].astype(jnp.float32)
        return jnp.where(inside, block, 0.0)

    position = lax.broadcasted_iota(jnp.int32, (width, channels), 0)

    def put(r, line, left, right):
        before = jnp.where(position == 0, left, pltpu.roll(line, 1, 0))
        behind = jnp.where(position == width - 1, right, pltpu.roll(line, width - 1, 0))
        cat[r, :, 0:channels] = before.astype(cat.dtype)
        cat[r, :, channels : 2 * channels] = line.astype(cat.dtype)
        cat[r, :, 2 * channels : 3 * channels] = behind.astype(cat.dtype)

    cols[0] = arrived(0, -1)
    cols[1] = arrived(0, 1)
    for dr, r in ((-1, 0), (1, height + 1)):
        put(r, arrived(dr, 0), arrived(dr, -1)[width - 1 : width], arrived(dr, 1)[0:1])

    def inner(r):
        put(r + 1, cells[r].astype(jnp.float32), cols[0, pl.ds(r, 1), :], cols[1, pl.ds(r, 1), :])

    loop(0, height, inner)


def windows(cat, start, rows):
    width, channels = cat.shape[1:]
    return jnp.concatenate(
        [cat[pl.ds(start + a, rows)].reshape(rows * width, channels) for a in range(3)], axis=1
    )


def over_cells(errors, field):
    return lax.dot_general(errors, field, (((0,), (0,)), ((), ())), preferred_element_type=jnp.float32)


def kernel(sizes, block_rows, data, params, scenes_hbm, cotangent_hbm, out,
           scenes, cotangent, edges, halo, cat_in, cat_err, cols, flat, ones, flipped, acc_one, acc_two, whole, local,
           own, square, squares, mine,
           theirs, sums, landed, kept, reached, theirs_b, sums_b, landed_b, kept_b, reached_b,
           load_sem, own_sem,
           sq_send, sq_recv, gather_send, row_gather, plane_gather, relay_send, relay_recv, halo_send, halo_recv,
           swap_send, swap_recv, plane_send, plane_recv, row_send, row_recv,
           swap_send_b, swap_recv_b, plane_send_b, plane_recv_b, row_send_b, row_recv_b):
    place = Place(sizes)
    n, me, half = place.n, place.me, place.half
    height, width, channels = scenes.shape
    rows = params.shape[0]
    taps = 9

    loads = [
        pltpu.make_async_copy(scenes_hbm, scenes, load_sem.at[0]),
        pltpu.make_async_copy(cotangent_hbm, cotangent, load_sem.at[1]),
    ]
    for load in loads:
        load.start()

    def load_own(j):
        chip = place.order(j)
        return pltpu.make_async_copy(data.at[chip, half], own.at[chip], own_sem.at[j])

    loop(0, n, lambda j: load_own(j).start())
    barrier = greet_all(place)
    for which, (load, cells) in enumerate(zip(loads, (scenes, cotangent))):
        load.wait()
        edges[0, which] = cells[0]
        edges[1, which] = cells[height - 1]
        edges[2, which] = cells[:, 0:16, :].astype(jnp.float32)[:, 0, :].astype(edges.dtype)
        edges[3, which] = cells[:, width - 16 : width, :].astype(jnp.float32)[:, 15, :].astype(edges.dtype)
    pl.semaphore_wait(barrier, 2 * n - 1)

    def loaded(j, chip):
        load_own(j).wait()
        return own[chip]

    start_halo(sizes, edges, halo, halo_send, halo_recv)
    grads = scatter_sum(
        place, data, loaded, theirs, sums, landed, kept, reached,
        swap_send, swap_recv, plane_send, plane_recv, row_send, row_recv,
    )

    square[...] = jnp.full(square.shape, jnp.sum(grads * grads), jnp.float32)

    def tell(chip, to_half, slot):
        pltpu.make_async_remote_copy(
            src_ref=square.at[0],
            dst_ref=squares.at[slot],
            send_sem=sq_send,
            recv_sem=sq_recv,
            device_id=place.device(chip, to_half),
            device_id_type=MESH,
        ).start()

    def tell_chip(j):
        chip = place.after(j)
        tell(chip, half, 2 * j - 1)
        tell(chip, 1 - half, 2 * j)

    loop(1, n, tell_chip)
    tell(me, 1 - half, 0)

    wait_all(halo, halo_recv)
    fill(sizes, 0, scenes, halo, cat_in, cols)
    fill(sizes, 1, cotangent, halo, cat_err, cols)

    wait_all(squares, sq_recv)
    norm2 = square[0] + jnp.sum(squares[...], axis=0)
    factor = radius / (jnp.sqrt(norm2) + epsilon)
    mine[...] = (params[...] + factor * grads).astype(mine.dtype)
    whole[me, half] = mine[...]

    def relay(src, chip):
        return pltpu.make_async_remote_copy(
            src_ref=src,
            dst_ref=whole.at[chip, half],
            send_sem=relay_send,
            recv_sem=relay_recv,
            device_id=place.device(me, 1 - half),
            device_id_type=MESH,
        )

    m, lines = place.m, place.rows

    def line_before(t):
        return lax.rem(place.row + 2 * lines - 1 - t, lines)

    def give_row(t):
        return pltpu.make_async_remote_copy(
            src_ref=mine,
            dst_ref=whole.at[me, half],
            send_sem=gather_send,
            recv_sem=row_gather.at[t],
            device_id=place.device(place.chip(place.plane, place.row_after(t)), half),
            device_id_type=MESH,
        )

    def give_plane(src, chip, t, u):
        return pltpu.make_async_remote_copy(
            src_ref=src,
            dst_ref=whole.at[chip, half],
            send_sem=gather_send,
            recv_sem=plane_gather.at[t * (m - 1) + u],
            device_id=place.device(place.chip(place.plane_after(u), place.row), half),
            device_id_type=MESH,
        )

    loop(0, lines - 1, lambda t: give_row(t).start())
    loop(0, m - 1, lambda u: give_plane(mine, me, lines - 1, u).start())
    relay(mine, me).start()

    def from_row(t):
        chip = place.chip(place.plane, line_before(t))
        give_row(t).wait_recv()
        loop(0, m - 1, lambda u: give_plane(whole.at[chip, half], chip, t, u).start())
        relay(whole.at[chip, half], chip).start()

    loop(0, lines - 1, from_row)

    def from_plane(i):
        t = lax.rem(i + lines - 1, lines)

        def arrival(u):
            chip = place.chip(lax.rem(place.plane + 2 * m - 1 - u, m), line_before(t))
            give_plane(mine, chip, t, u).wait_recv()
            relay(whole.at[chip, half], chip).start()

        loop(0, m - 1, arrival)

    loop(0, lines, from_plane)
    wait_all(whole.at[:, 0], relay_recv)
    wait_all(whole.at[:, 0], relay_send)
    wait_all(whole.at[pl.ds(0, n - 1), 0], gather_send)
    wait_all(squares, sq_send)
    wait_all(halo, halo_send)

    def spread(c):
        flat[pl.ds(c * rows, rows), :] = whole[c // 2, lax.rem(c, 2)].astype(jnp.float32)

    loop(0, 2 * n, spread)
    ones[...] = flat[0 : taps * channels].astype(ones.dtype)
    for t in range(taps):
        first = (2 * taps - 1 - t) * channels
        flipped[t * channels : (t + 1) * channels] = flat[first : first + channels].T.astype(flipped.dtype)
    acc_one[...] = jnp.zeros_like(acc_one)
    acc_two[...] = jnp.zeros_like(acc_two)

    def step(i):
        start = i * block_rows
        fields = windows(cat_in, start, block_rows)
        errors = windows(cat_err, start, block_rows)
        pre = jnp.dot(fields, ones[...], preferred_element_type=jnp.float32)
        back = jnp.dot(errors, flipped[...], preferred_element_type=jnp.float32)
        squash = jax.nn.sigmoid(pre)
        hidden = (pre * squash).astype(jnp.bfloat16)
        delta = (back * squash * (1.0 + pre * (1.0 - squash))).astype(jnp.bfloat16)
        acc_one[...] += over_cells(delta, fields)
        acc_two[...] += over_cells(hidden, errors)

    loop(0, height // block_rows, step)
    for t in range(taps):
        flat[t * channels : (t + 1) * channels] = acc_one[:, t * channels : (t + 1) * channels].T
        u = taps - 1 - t
        flat[(taps + t) * channels : (taps + t + 1) * channels] = acc_two[:, u * channels : (u + 1) * channels]

    def collect(c):
        local[c // 2, lax.rem(c, 2)] = flat[pl.ds(c * rows, rows), :]

    loop(0, 2 * n, collect)
    out[...] = scatter_sum(
        place, local, lambda j, chip: local[chip, half], theirs_b, sums_b, landed_b, kept_b, reached_b,
        swap_send_b, swap_recv_b, plane_send_b, plane_recv_b, row_send_b, row_recv_b,
    )


def on_device(sizes, scenes, cotangent, params, partials):
    scenes, cotangent = scenes[0], cotangent[0]
    height, width, channels = scenes.shape
    n = sizes[0] * sizes[1] * sizes[2] // 2
    rows = params.size // LANES
    dma = pltpu.SemaphoreType.DMA
    half_type, full = jnp.bfloat16, jnp.float32
    anywhere, vmem = pl.BlockSpec(memory_space=pl.ANY), pl.BlockSpec(memory_space=pltpu.VMEM)
    cat = pltpu.VMEM((height + 2, width, 3 * channels), half_type)
    tall = pltpu.VMEM((9 * channels, channels), half_type)
    acc = pltpu.VMEM((channels, 9 * channels), full)
    lines, m = sizes[1], n // sizes[1]
    chunks = [
        pltpu.VMEM((n, rows, LANES), full),
        pltpu.VMEM((n - lines, rows, LANES), half_type),
        pltpu.VMEM((lines, m - 1, rows, LANES), half_type),
        pltpu.VMEM((lines, rows, LANES), full),
        pltpu.VMEM((lines - 1, rows, LANES), full),
    ]
    sum_sems = [dma, dma((n,)), dma, dma((lines,)), dma, dma]
    scratch = [
        pltpu.VMEM(scenes.shape, half_type),
        pltpu.VMEM(scenes.shape, half_type),
        pltpu.VMEM((4, 2, width, channels), half_type),
        pltpu.VMEM((len(AROUND), 2, width, channels), half_type),
        cat,
        cat,
        pltpu.VMEM((2, height, channels), full),
        pltpu.VMEM((18 * channels, channels), full),
        tall,
        tall,
        acc,
        acc,
        pltpu.VMEM((n, 2, rows, LANES), half_type),
        pltpu.VMEM((n, 2, rows, LANES), full),
        pltpu.VMEM((n, rows, LANES), full),
        pltpu.VMEM((1, 1, LANES), full),
        pltpu.VMEM((2 * n - 1, 1, LANES), full),
        pltpu.VMEM((rows, LANES), half_type),
        *chunks,
        *chunks,
        dma((2,)), dma((n,)),
        dma, dma, dma, dma((lines - 1,)), dma((n - lines,)), dma, dma, dma, dma,
        *sum_sems,
        *sum_sems,
    ]
    grads = pl.pallas_call(
        functools.partial(kernel, sizes, 8),
        out_shape=jax.ShapeDtypeStruct((rows, LANES), full),
        in_specs=[anywhere, vmem, anywhere, anywhere],
        out_specs=vmem,
        scratch_shapes=scratch,
        compiler_params=pltpu.CompilerParams(
            collective_id=0, has_side_effects=True, vmem_limit_bytes=56 * 2**20
        ),
        name="sam_grad",
    )(partials[0].reshape(n, 2, rows, LANES), params.reshape(rows, LANES), scenes, cotangent)
    return grads.reshape(-1)


def solution(mesh):
    sizes = tuple(mesh.shape[axis] for axis in AXES)
    return jax.shard_map(
        functools.partial(on_device, sizes),
        mesh=mesh,
        in_specs=(
            P("scene", "row", "col", None),
            P("scene", "row", "col", None),
            P(AXES),
            P(AXES, None),
        ),
        out_specs=P(AXES),
        check_vma=False,
    )
```

```python
import functools

import jax
import jax.numpy as jnp
from jax import lax
from jax.experimental import pallas as pl
from jax.experimental.pallas import tpu as pltpu
from jax.sharding import PartitionSpec as P

radius = 2.0
epsilon = 1e-06
AXES = ("scene", "row", "col")
MESH = pl.DeviceIdType.MESH
LANES = 128


class Place:
    def __init__(self, sizes):
        self.scenes, self.rows, self.cols = sizes
        self.pairs = self.cols // 2
        self.n = self.scenes * self.rows * self.pairs
        col = lax.axis_index("col")
        self.half = lax.rem(col, 2)
        self.m = self.scenes * self.pairs
        self.row = lax.axis_index("row")
        self.plane = lax.axis_index("scene") * self.pairs + col // 2
        self.me = self.chip(self.plane, self.row)

    def chip(self, plane, row):
        return (plane // self.pairs * self.rows + row) * self.pairs + lax.rem(plane, self.pairs)

    def plane_after(self, u):
        return lax.rem(self.plane + 1 + u, self.m)

    def row_after(self, t):
        return lax.rem(self.row + 1 + t, self.rows)

    def order(self, j):
        return self.chip(self.plane_after(lax.rem(j, self.m)), self.row_after(j // self.m))

    def device(self, chip, half):
        return {
            "scene": chip // (self.rows * self.pairs),
            "row": lax.rem(chip // self.pairs, self.rows),
            "col": lax.rem(chip, self.pairs) * 2 + half,
        }

    def after(self, step):
        return lax.rem(self.me + step, self.n)


def loop(low, high, body, unroll=1):
    def wrapped(j, carry):
        body(j)
        return carry

    lax.fori_loop(low, high, wrapped, 0, unroll=unroll)


def wait_all(ref, sem):
    pltpu.make_async_copy(ref, ref, sem).wait()


def greet_all(place):
    barrier = pltpu.get_barrier_semaphore()

    def greet(j):
        chip = place.after(j)
        pl.semaphore_signal(barrier, inc=1, device_id=place.device(chip, place.half), device_id_type=MESH)
        pl.semaphore_signal(barrier, inc=1, device_id=place.device(chip, 1 - place.half), device_id_type=MESH)

    pl.semaphore_signal(barrier, inc=1, device_id=place.device(place.me, 1 - place.half), device_id_type=MESH)
    loop(1, place.n, greet)
    return barrier


def scatter_sum(place, data, own, theirs, sums, landed, kept, reached,
                swap_send, swap_recv, plane_send, plane_recv, row_send, row_recv):
    n, m, rows, me, half = place.n, place.m, place.rows, place.me, place.half
    full = jnp.float32

    def swap(j):
        chip = place.order(j)
        return pltpu.make_async_remote_copy(
            src_ref=data.at[chip, 1 - half],
            dst_ref=theirs.at[chip],
            send_sem=swap_send,
            recv_sem=swap_recv.at[j],
            device_id=place.device(me, 1 - half),
            device_id_type=MESH,
        )

    loop(0, n, lambda j: swap(j).start())

    def both(j):
        chip = place.order(j)
        mine = own(j, chip)
        swap(j).wait_recv()
        return mine + theirs[chip]

    def across_plane(t):
        def pass_on(u):
            slot = t * (m - 1) + u
            sums[slot] = both(t * m + u).astype(sums.dtype)
            pltpu.make_async_remote_copy(
                src_ref=sums.at[slot],
                dst_ref=landed.at[t, u],
                send_sem=plane_send,
                recv_sem=plane_recv.at[t],
                device_id=place.device(place.chip(place.plane_after(u), place.row), half),
                device_id_type=MESH,
            ).start()

        loop(0, m - 1, pass_on)
        kept[t] = both(t * m + m - 1)

    loop(0, rows, across_plane)

    def plane_total(t):
        wait_all(landed.at[t], plane_recv.at[t])
        return lax.fori_loop(0, m - 1, lambda u, sofar: sofar + landed[t, u].astype(full), kept[t])

    def along_rows(t):
        kept[t] = plane_total(t)
        pltpu.make_async_remote_copy(
            src_ref=kept.at[t],
            dst_ref=reached.at[t],
            send_sem=row_send,
            recv_sem=row_recv,
            device_id=place.device(place.chip(place.plane, place.row_after(t)), half),
            device_id_type=MESH,
        ).start()

    loop(0, rows - 1, along_rows)
    total = plane_total(rows - 1)
    wait_all(reached, row_recv)
    total = lax.fori_loop(0, rows - 1, lambda t, sofar: sofar + reached[t], total)
    wait_all(theirs, swap_send)
    wait_all(sums, plane_send)
    wait_all(reached, row_send)
    return total


AROUND = tuple((dr, dc) for dr in (-1, 0, 1) for dc in (-1, 0, 1) if dr or dc)


def edge_of(dr, dc):
    if dr:
        return 1 if dr < 0 else 0
    return 3 if dc < 0 else 2


def start_halo(sizes, edges, halo, halo_send, halo_recv):
    row, col = lax.axis_index("row"), lax.axis_index("col")
    for slot, (dr, dc) in enumerate(AROUND):
        pltpu.make_async_remote_copy(
            src_ref=edges.at[edge_of(dr, dc)],
            dst_ref=halo.at[slot],
            send_sem=halo_send,
            recv_sem=halo_recv,
            device_id={
                "scene": lax.axis_index("scene"),
                "row": lax.rem(row + sizes[1] - dr, sizes[1]),
                "col": lax.rem(col + sizes[2] - dc, sizes[2]),
            },
            device_id_type=MESH,
        ).start()


def fill(sizes, which, cells, halo, cat, cols):
    height, width, channels = cells.shape
    row, col = lax.axis_index("row"), lax.axis_index("col")
    inside_row = {-1: row > 0, 0: row >= 0, 1: row < sizes[1] - 1}
    inside_col = {-1: col > 0, 0: col >= 0, 1: col < sizes[2] - 1}

    def arrived(dr, dc):
        inside = jnp.logical_and(inside_row[dr], inside_col[dc])
        block = halo[AROUND.index((dr, dc)), which].astype(jnp.float32)
        return jnp.where(inside, block, 0.0)

    position = lax.broadcasted_iota(jnp.int32, (width, channels), 0)

    def put(r, line, left, right):
        before = jnp.where(position == 0, left, pltpu.roll(line, 1, 0))
        behind = jnp.where(position == width - 1, right, pltpu.roll(line, width - 1, 0))
        cat[r, :, 0:channels] = before.astype(cat.dtype)
        cat[r, :, channels : 2 * channels] = line.astype(cat.dtype)
        cat[r, :, 2 * channels : 3 * channels] = behind.astype(cat.dtype)

    cols[0] = arrived(0, -1)
    cols[1] = arrived(0, 1)
    for dr, r in ((-1, 0), (1, height + 1)):
        put(r, arrived(dr, 0), arrived(dr, -1)[width - 1 : width], arrived(dr, 1)[0:1])

    def inner(r):
        put(r + 1, cells[r].astype(jnp.float32), cols[0, pl.ds(r, 1), :], cols[1, pl.ds(r, 1), :])

    loop(0, height, inner, unroll=4)


def windows(cat, start, rows):
    width, channels = cat.shape[1:]
    return jnp.concatenate(
        [cat[pl.ds(start + a, rows)].reshape(rows * width, channels) for a in range(3)], axis=1
    )


def over_cells(errors, field):
    return lax.dot_general(errors, field, (((0,), (0,)), ((), ())), preferred_element_type=jnp.float32)


def kernel(sizes, block_rows, data, params, scenes_hbm, cotangent_hbm, out,
           scenes, cotangent, edges, halo, cat_in, cat_err, cols, flat, ones, flipped, acc_one, acc_two, whole, local,
           own, square, squares, mine,
           theirs, sums, landed, kept, reached, theirs_b, sums_b, landed_b, kept_b, reached_b,
           load_sem, own_sem,
           sq_send, sq_recv, gather_send, row_gather, plane_gather, relay_send, relay_recv, halo_send, halo_recv,
           swap_send, swap_recv, plane_send, plane_recv, row_send, row_recv,
           swap_send_b, swap_recv_b, plane_send_b, plane_recv_b, row_send_b, row_recv_b):
    place = Place(sizes)
    n, me, half = place.n, place.me, place.half
    height, width, channels = scenes.shape
    rows = params.shape[0]
    taps = 9

    loads = [
        pltpu.make_async_copy(scenes_hbm, scenes, load_sem.at[0]),
        pltpu.make_async_copy(cotangent_hbm, cotangent, load_sem.at[1]),
    ]
    for load in loads:
        load.start()

    def load_own(j):
        chip = place.order(j)
        return pltpu.make_async_copy(data.at[chip, half], own.at[chip], own_sem.at[j])

    loop(0, n, lambda j: load_own(j).start())
    barrier = greet_all(place)
    for which, (load, cells) in enumerate(zip(loads, (scenes, cotangent))):
        load.wait()
        edges[0, which] = cells[0]
        edges[1, which] = cells[height - 1]
        edges[2, which] = cells[:, 0:16, :].astype(jnp.float32)[:, 0, :].astype(edges.dtype)
        edges[3, which] = cells[:, width - 16 : width, :].astype(jnp.float32)[:, 15, :].astype(edges.dtype)
    pl.semaphore_wait(barrier, 2 * n - 1)

    def loaded(j, chip):
        load_own(j).wait()
        return own[chip]

    start_halo(sizes, edges, halo, halo_send, halo_recv)
    grads = scatter_sum(
        place, data, loaded, theirs, sums, landed, kept, reached,
        swap_send, swap_recv, plane_send, plane_recv, row_send, row_recv,
    )

    square[...] = jnp.full(square.shape, jnp.sum(grads * grads), jnp.float32)

    def tell(chip, to_half, slot):
        pltpu.make_async_remote_copy(
            src_ref=square.at[0],
            dst_ref=squares.at[slot],
            send_sem=sq_send,
            recv_sem=sq_recv,
            device_id=place.device(chip, to_half),
            device_id_type=MESH,
        ).start()

    def tell_chip(j):
        chip = place.after(j)
        tell(chip, half, 2 * j - 1)
        tell(chip, 1 - half, 2 * j)

    loop(1, n, tell_chip)
    tell(me, 1 - half, 0)

    wait_all(halo, halo_recv)
    fill(sizes, 0, scenes, halo, cat_in, cols)

    wait_all(squares, sq_recv)
    norm2 = square[0] + jnp.sum(squares[...], axis=0)
    factor = radius / (jnp.sqrt(norm2) + epsilon)
    mine[...] = (params[...] + factor * grads).astype(mine.dtype)
    whole[me, half] = mine[...]

    def relay(src, chip):
        return pltpu.make_async_remote_copy(
            src_ref=src,
            dst_ref=whole.at[chip, half],
            send_sem=relay_send,
            recv_sem=relay_recv,
            device_id=place.device(me, 1 - half),
            device_id_type=MESH,
        )

    m, lines = place.m, place.rows

    def line_before(t):
        return lax.rem(place.row + 2 * lines - 1 - t, lines)

    def give_row(t):
        return pltpu.make_async_remote_copy(
            src_ref=mine,
            dst_ref=whole.at[me, half],
            send_sem=gather_send,
            recv_sem=row_gather.at[t],
            device_id=place.device(place.chip(place.plane, place.row_after(t)), half),
            device_id_type=MESH,
        )

    def give_plane(src, chip, t, u):
        return pltpu.make_async_remote_copy(
            src_ref=src,
            dst_ref=whole.at[chip, half],
            send_sem=gather_send,
            recv_sem=plane_gather.at[t * (m - 1) + u],
            device_id=place.device(place.chip(place.plane_after(u), place.row), half),
            device_id_type=MESH,
        )

    loop(0, lines - 1, lambda t: give_row(t).start())
    loop(0, m - 1, lambda u: give_plane(mine, me, lines - 1, u).start())
    relay(mine, me).start()
    fill(sizes, 1, cotangent, halo, cat_err, cols)

    def from_row(t):
        chip = place.chip(place.plane, line_before(t))
        give_row(t).wait_recv()
        loop(0, m - 1, lambda u: give_plane(whole.at[chip, half], chip, t, u).start())
        relay(whole.at[chip, half], chip).start()

    loop(0, lines - 1, from_row)

    def from_plane(i):
        t = lax.rem(i + lines - 1, lines)

        def arrival(u):
            chip = place.chip(lax.rem(place.plane + 2 * m - 1 - u, m), line_before(t))
            give_plane(mine, chip, t, u).wait_recv()
            relay(whole.at[chip, half], chip).start()

        loop(0, m - 1, arrival)

    loop(0, lines, from_plane)
    wait_all(whole.at[:, 0], relay_recv)
    wait_all(whole.at[:, 0], relay_send)
    wait_all(whole.at[pl.ds(0, n - 1), 0], gather_send)
    wait_all(squares, sq_send)
    wait_all(halo, halo_send)

    def spread(c):
        flat[pl.ds(c * rows, rows), :] = whole[c // 2, lax.rem(c, 2)].astype(jnp.float32)

    loop(0, 2 * n, spread, unroll=4)
    ones[...] = flat[0 : taps * channels].astype(ones.dtype)
    for t in range(taps):
        first = (2 * taps - 1 - t) * channels
        flipped[t * channels : (t + 1) * channels] = flat[first : first + channels].T.astype(flipped.dtype)
    acc_one[...] = jnp.zeros_like(acc_one)
    acc_two[...] = jnp.zeros_like(acc_two)

    def step(i):
        start = i * block_rows
        fields = windows(cat_in, start, block_rows)
        errors = windows(cat_err, start, block_rows)
        pre = jnp.dot(fields, ones[...], preferred_element_type=jnp.float32)
        back = jnp.dot(errors, flipped[...], preferred_element_type=jnp.float32)
        squash = jax.nn.sigmoid(pre)
        hidden = (pre * squash).astype(jnp.bfloat16)
        delta = (back * squash * (1.0 + pre * (1.0 - squash))).astype(jnp.bfloat16)
        acc_one[...] += over_cells(delta, fields)
        acc_two[...] += over_cells(hidden, errors)

    loop(0, height // block_rows, step)
    for t in range(taps):
        flat[t * channels : (t + 1) * channels] = acc_one[:, t * channels : (t + 1) * channels].T
        u = taps - 1 - t
        flat[(taps + t) * channels : (taps + t + 1) * channels] = acc_two[:, u * channels : (u + 1) * channels]

    def collect(c):
        local[c // 2, lax.rem(c, 2)] = flat[pl.ds(c * rows, rows), :]

    loop(0, 2 * n, collect, unroll=4)
    out[...] = scatter_sum(
        place, local, lambda j, chip: local[chip, half], theirs_b, sums_b, landed_b, kept_b, reached_b,
        swap_send_b, swap_recv_b, plane_send_b, plane_recv_b, row_send_b, row_recv_b,
    )


def on_device(sizes, scenes, cotangent, params, partials):
    scenes, cotangent = scenes[0], cotangent[0]
    height, width, channels = scenes.shape
    n = sizes[0] * sizes[1] * sizes[2] // 2
    rows = params.size // LANES
    dma = pltpu.SemaphoreType.DMA
    half_type, full = jnp.bfloat16, jnp.float32
    anywhere, vmem = pl.BlockSpec(memory_space=pl.ANY), pl.BlockSpec(memory_space=pltpu.VMEM)
    cat = pltpu.VMEM((height + 2, width, 3 * channels), half_type)
    tall = pltpu.VMEM((9 * channels, channels), half_type)
    acc = pltpu.VMEM((channels, 9 * channels), full)
    lines, m = sizes[1], n // sizes[1]
    chunks = [
        pltpu.VMEM((n, rows, LANES), full),
        pltpu.VMEM((n - lines, rows, LANES), half_type),
        pltpu.VMEM((lines, m - 1, rows, LANES), half_type),
        pltpu.VMEM((lines, rows, LANES), full),
        pltpu.VMEM((lines - 1, rows, LANES), full),
    ]
    sum_sems = [dma, dma((n,)), dma, dma((lines,)), dma, dma]
    scratch = [
        pltpu.VMEM(scenes.shape, half_type),
        pltpu.VMEM(scenes.shape, half_type),
        pltpu.VMEM((4, 2, width, channels), half_type),
        pltpu.VMEM((len(AROUND), 2, width, channels), half_type),
        cat,
        cat,
        pltpu.VMEM((2, height, channels), full),
        pltpu.VMEM((18 * channels, channels), full),
        tall,
        tall,
        acc,
        acc,
        pltpu.VMEM((n, 2, rows, LANES), half_type),
        pltpu.VMEM((n, 2, rows, LANES), full),
        pltpu.VMEM((n, rows, LANES), full),
        pltpu.VMEM((1, 1, LANES), full),
        pltpu.VMEM((2 * n - 1, 1, LANES), full),
        pltpu.VMEM((rows, LANES), half_type),
        *chunks,
        *chunks,
        dma((2,)), dma((n,)),
        dma, dma, dma, dma((lines - 1,)), dma((n - lines,)), dma, dma, dma, dma,
        *sum_sems,
        *sum_sems,
    ]
    grads = pl.pallas_call(
        functools.partial(kernel, sizes, 8),
        out_shape=jax.ShapeDtypeStruct((rows, LANES), full),
        in_specs=[anywhere, vmem, anywhere, anywhere],
        out_specs=vmem,
        scratch_shapes=scratch,
        compiler_params=pltpu.CompilerParams(
            collective_id=0, has_side_effects=True, vmem_limit_bytes=56 * 2**20
        ),
        name="sam_grad",
    )(partials[0].reshape(n, 2, rows, LANES), params.reshape(rows, LANES), scenes, cotangent)
    return grads.reshape(-1)


def solution(mesh):
    sizes = tuple(mesh.shape[axis] for axis in AXES)
    return jax.shard_map(
        functools.partial(on_device, sizes),
        mesh=mesh,
        in_specs=(
            P("scene", "row", "col", None),
            P("scene", "row", "col", None),
            P(AXES),
            P(AXES, None),
        ),
        out_specs=P(AXES),
        check_vma=False,
    )
```

```python
import functools

import jax
import jax.numpy as jnp
from jax import lax
from jax.experimental import pallas as pl
from jax.experimental.pallas import tpu as pltpu
from jax.sharding import PartitionSpec as P

radius = 2.0
epsilon = 1e-06
AXES = ("scene", "row", "col")
MESH = pl.DeviceIdType.MESH
LANES = 128


class Place:
    def __init__(self, sizes):
        self.scenes, self.rows, self.cols = sizes
        self.pairs = self.cols // 2
        self.n = self.scenes * self.rows * self.pairs
        col = lax.axis_index("col")
        self.half = lax.rem(col, 2)
        self.m = self.scenes * self.pairs
        self.row = lax.axis_index("row")
        self.plane = lax.axis_index("scene") * self.pairs + col // 2
        self.me = self.chip(self.plane, self.row)

    def chip(self, plane, row):
        return (plane // self.pairs * self.rows + row) * self.pairs + lax.rem(plane, self.pairs)

    def plane_after(self, u):
        return lax.rem(self.plane + 1 + u, self.m)

    def row_after(self, t):
        return lax.rem(self.row + 1 + t, self.rows)

    def order(self, j):
        return self.chip(self.plane_after(lax.rem(j, self.m)), self.row_after(j // self.m))

    def device(self, chip, half):
        return {
            "scene": chip // (self.rows * self.pairs),
            "row": lax.rem(chip // self.pairs, self.rows),
            "col": lax.rem(chip, self.pairs) * 2 + half,
        }

    def after(self, step):
        return lax.rem(self.me + step, self.n)


def loop(low, high, body, unroll=1):
    def wrapped(j, carry):
        body(j)
        return carry

    lax.fori_loop(low, high, wrapped, 0, unroll=unroll)


def wait_all(ref, sem):
    pltpu.make_async_copy(ref, ref, sem).wait()


def greet_all(place):
    barrier = pltpu.get_barrier_semaphore()

    def greet(j):
        chip = place.after(j)
        pl.semaphore_signal(barrier, inc=1, device_id=place.device(chip, place.half), device_id_type=MESH)
        pl.semaphore_signal(barrier, inc=1, device_id=place.device(chip, 1 - place.half), device_id_type=MESH)

    pl.semaphore_signal(barrier, inc=1, device_id=place.device(place.me, 1 - place.half), device_id_type=MESH)
    loop(1, place.n, greet)
    return barrier


def scatter_sum(place, data, own, theirs, sums, landed, kept, reached,
                swap_send, swap_recv, plane_send, plane_recv, row_send, row_recv):
    n, m, rows, me, half = place.n, place.m, place.rows, place.me, place.half
    full = jnp.float32

    def swap(j):
        chip = place.order(j)
        return pltpu.make_async_remote_copy(
            src_ref=data.at[chip, 1 - half],
            dst_ref=theirs.at[chip],
            send_sem=swap_send,
            recv_sem=swap_recv.at[j],
            device_id=place.device(me, 1 - half),
            device_id_type=MESH,
        )

    loop(0, n, lambda j: swap(j).start())

    def both(j):
        chip = place.order(j)
        mine = own(j, chip)
        swap(j).wait_recv()
        return mine + theirs[chip]

    def across_plane(t):
        def pass_on(u):
            slot = t * (m - 1) + u
            sums[slot] = both(t * m + u).astype(sums.dtype)
            pltpu.make_async_remote_copy(
                src_ref=sums.at[slot],
                dst_ref=landed.at[t, u],
                send_sem=plane_send,
                recv_sem=plane_recv.at[t],
                device_id=place.device(place.chip(place.plane_after(u), place.row), half),
                device_id_type=MESH,
            ).start()

        loop(0, m - 1, pass_on)
        kept[t] = both(t * m + m - 1)

    loop(0, rows, across_plane)

    def plane_total(t):
        wait_all(landed.at[t], plane_recv.at[t])
        return lax.fori_loop(0, m - 1, lambda u, sofar: sofar + landed[t, u].astype(full), kept[t])

    def along_rows(t):
        kept[t] = plane_total(t)
        pltpu.make_async_remote_copy(
            src_ref=kept.at[t],
            dst_ref=reached.at[t],
            send_sem=row_send,
            recv_sem=row_recv,
            device_id=place.device(place.chip(place.plane, place.row_after(t)), half),
            device_id_type=MESH,
        ).start()

    loop(0, rows - 1, along_rows)
    total = plane_total(rows - 1)
    wait_all(reached, row_recv)
    total = lax.fori_loop(0, rows - 1, lambda t, sofar: sofar + reached[t], total)
    wait_all(theirs, swap_send)
    wait_all(sums, plane_send)
    wait_all(reached, row_send)
    return total


AROUND = tuple((dr, dc) for dr in (-1, 0, 1) for dc in (-1, 0, 1) if dr or dc)


def edge_of(dr, dc):
    if dr:
        return 1 if dr < 0 else 0
    return 3 if dc < 0 else 2


def start_halo(sizes, edges, halo, halo_send, halo_recv):
    row, col = lax.axis_index("row"), lax.axis_index("col")
    for slot, (dr, dc) in enumerate(AROUND):
        pltpu.make_async_remote_copy(
            src_ref=edges.at[edge_of(dr, dc)],
            dst_ref=halo.at[slot],
            send_sem=halo_send,
            recv_sem=halo_recv,
            device_id={
                "scene": lax.axis_index("scene"),
                "row": lax.rem(row + sizes[1] - dr, sizes[1]),
                "col": lax.rem(col + sizes[2] - dc, sizes[2]),
            },
            device_id_type=MESH,
        ).start()


def fill(sizes, which, cells, halo, cat, cols):
    height, width, channels = cells.shape
    row, col = lax.axis_index("row"), lax.axis_index("col")
    inside_row = {-1: row > 0, 0: row >= 0, 1: row < sizes[1] - 1}
    inside_col = {-1: col > 0, 0: col >= 0, 1: col < sizes[2] - 1}

    def arrived(dr, dc):
        inside = jnp.logical_and(inside_row[dr], inside_col[dc])
        block = halo[AROUND.index((dr, dc)), which].astype(jnp.float32)
        return jnp.where(inside, block, 0.0)

    position = lax.broadcasted_iota(jnp.int32, (width, channels), 0)

    def put(r, line, left, right):
        before = jnp.where(position == 0, left, pltpu.roll(line, 1, 0))
        behind = jnp.where(position == width - 1, right, pltpu.roll(line, width - 1, 0))
        cat[r, :, 0:channels] = before.astype(cat.dtype)
        cat[r, :, channels : 2 * channels] = line.astype(cat.dtype)
        cat[r, :, 2 * channels : 3 * channels] = behind.astype(cat.dtype)

    cols[0] = arrived(0, -1)
    cols[1] = arrived(0, 1)
    for dr, r in ((-1, 0), (1, height + 1)):
        put(r, arrived(dr, 0), arrived(dr, -1)[width - 1 : width], arrived(dr, 1)[0:1])

    def inner(r):
        put(r + 1, cells[r].astype(jnp.float32), cols[0, pl.ds(r, 1), :], cols[1, pl.ds(r, 1), :])

    loop(0, height, inner, unroll=4)


def windows(cat, start, rows):
    width, channels = cat.shape[1:]
    return jnp.concatenate(
        [cat[pl.ds(start + a, rows)].reshape(rows * width, channels) for a in range(3)], axis=1
    )


def over_cells(errors, field):
    return lax.dot_general(errors, field, (((0,), (0,)), ((), ())), preferred_element_type=jnp.float32)


def kernel(sizes, block_rows, data, params, scenes_hbm, cotangent_hbm, out,
           scenes, cotangent, edges, halo, cat_in, cat_err, cols, flat, ones, flipped, acc_one, acc_two, whole, local,
           own, square, squares, mine,
           theirs, sums, landed, kept, reached, theirs_b, sums_b, landed_b, kept_b, reached_b,
           load_sem, own_sem,
           sq_send, sq_recv, gather_send, row_gather, plane_gather, relay_send, relay_recv, halo_send, halo_recv,
           swap_send, swap_recv, plane_send, plane_recv, row_send, row_recv,
           swap_send_b, swap_recv_b, plane_send_b, plane_recv_b, row_send_b, row_recv_b):
    place = Place(sizes)
    n, me, half = place.n, place.me, place.half
    height, width, channels = scenes.shape
    rows = params.shape[0]
    taps = 9

    loads = [
        pltpu.make_async_copy(scenes_hbm, scenes, load_sem.at[0]),
        pltpu.make_async_copy(cotangent_hbm, cotangent, load_sem.at[1]),
    ]
    for load in loads:
        load.start()

    def load_own(j):
        chip = place.order(j)
        return pltpu.make_async_copy(data.at[chip, half], own.at[chip], own_sem.at[j])

    loop(0, n, lambda j: load_own(j).start())
    barrier = greet_all(place)
    for which, (load, cells) in enumerate(zip(loads, (scenes, cotangent))):
        load.wait()
        edges[0, which] = cells[0]
        edges[1, which] = cells[height - 1]
        edges[2, which] = cells[:, 0:16, :].astype(jnp.float32)[:, 0, :].astype(edges.dtype)
        edges[3, which] = cells[:, width - 16 : width, :].astype(jnp.float32)[:, 15, :].astype(edges.dtype)
    pl.semaphore_wait(barrier, 2 * n - 1)

    def loaded(j, chip):
        load_own(j).wait()
        return own[chip]

    start_halo(sizes, edges, halo, halo_send, halo_recv)
    grads = scatter_sum(
        place, data, loaded, theirs, sums, landed, kept, reached,
        swap_send, swap_recv, plane_send, plane_recv, row_send, row_recv,
    )

    square[...] = jnp.full(square.shape, jnp.sum(grads * grads), jnp.float32)

    def tell(chip, to_half, slot):
        pltpu.make_async_remote_copy(
            src_ref=square.at[0],
            dst_ref=squares.at[slot],
            send_sem=sq_send,
            recv_sem=sq_recv,
            device_id=place.device(chip, to_half),
            device_id_type=MESH,
        ).start()

    def tell_chip(j):
        chip = place.after(j)
        tell(chip, half, 2 * j - 1)
        tell(chip, 1 - half, 2 * j)

    loop(1, n, tell_chip)
    tell(me, 1 - half, 0)

    wait_all(halo, halo_recv)
    fill(sizes, 0, scenes, halo, cat_in, cols)

    wait_all(squares, sq_recv)
    norm2 = square[0] + jnp.sum(squares[...], axis=0)
    factor = radius / (jnp.sqrt(norm2) + epsilon)
    mine[...] = (params[...] + factor * grads).astype(mine.dtype)
    whole[me, half] = mine[...]

    def relay(src, chip):
        return pltpu.make_async_remote_copy(
            src_ref=src,
            dst_ref=whole.at[chip, half],
            send_sem=relay_send,
            recv_sem=relay_recv,
            device_id=place.device(me, 1 - half),
            device_id_type=MESH,
        )

    m, lines = place.m, place.rows

    def line_before(t):
        return lax.rem(place.row + 2 * lines - 1 - t, lines)

    def give_row(t):
        return pltpu.make_async_remote_copy(
            src_ref=mine,
            dst_ref=whole.at[me, half],
            send_sem=gather_send,
            recv_sem=row_gather.at[t],
            device_id=place.device(place.chip(place.plane, place.row_after(t)), half),
            device_id_type=MESH,
        )

    def give_plane(src, chip, t, u):
        return pltpu.make_async_remote_copy(
            src_ref=src,
            dst_ref=whole.at[chip, half],
            send_sem=gather_send,
            recv_sem=plane_gather.at[t * (m - 1) + u],
            device_id=place.device(place.chip(place.plane_after(u), place.row), half),
            device_id_type=MESH,
        )

    loop(0, lines - 1, lambda t: give_row(t).start())
    loop(0, m - 1, lambda u: give_plane(mine, me, lines - 1, u).start())
    relay(mine, me).start()
    fill(sizes, 1, cotangent, halo, cat_err, cols)

    def from_row(t):
        chip = place.chip(place.plane, line_before(t))
        give_row(t).wait_recv()
        loop(0, m - 1, lambda u: give_plane(whole.at[chip, half], chip, t, u).start())
        relay(whole.at[chip, half], chip).start()

    loop(0, lines - 1, from_row)

    def from_plane(i):
        t = lax.rem(i + lines - 1, lines)

        def arrival(u):
            chip = place.chip(lax.rem(place.plane + 2 * m - 1 - u, m), line_before(t))
            give_plane(mine, chip, t, u).wait_recv()
            relay(whole.at[chip, half], chip).start()

        loop(0, m - 1, arrival)

    loop(0, lines, from_plane)
    wait_all(whole.at[:, 0], relay_recv)
    wait_all(whole.at[:, 0], relay_send)
    wait_all(whole.at[pl.ds(0, n - 1), 0], gather_send)
    wait_all(squares, sq_send)
    wait_all(halo, halo_send)

    def spread(c):
        flat[pl.ds(c * rows, rows), :] = whole[c // 2, lax.rem(c, 2)].astype(jnp.float32)

    loop(0, 2 * n, spread, unroll=4)
    ones[...] = flat[0 : taps * channels].astype(ones.dtype)
    for t in range(taps):
        first = (2 * taps - 1 - t) * channels
        flipped[t * channels : (t + 1) * channels] = flat[first : first + channels].T.astype(flipped.dtype)
    acc_one[...] = jnp.zeros_like(acc_one)
    acc_two[...] = jnp.zeros_like(acc_two)

    def step(i):
        start = i * block_rows
        fields = windows(cat_in, start, block_rows)
        errors = windows(cat_err, start, block_rows)
        pre = jnp.dot(fields, ones[...], preferred_element_type=jnp.float32)
        back = jnp.dot(errors, flipped[...], preferred_element_type=jnp.float32)
        squash = jax.nn.sigmoid(pre)
        hidden = (pre * squash).astype(jnp.bfloat16)
        delta = (back * squash * (1.0 + pre * (1.0 - squash))).astype(jnp.bfloat16)
        acc_one[...] += over_cells(delta, fields)
        acc_two[...] += over_cells(hidden, errors)

    loop(0, height // block_rows, step)
    for t in range(taps):
        flat[t * channels : (t + 1) * channels] = acc_one[:, t * channels : (t + 1) * channels].T
        u = taps - 1 - t
        flat[(taps + t) * channels : (taps + t + 1) * channels] = acc_two[:, u * channels : (u + 1) * channels]

    def collect(c):
        local[c // 2, lax.rem(c, 2)] = flat[pl.ds(c * rows, rows), :]

    loop(0, 2 * n, collect, unroll=4)
    out[...] = scatter_sum(
        place, local, lambda j, chip: local[chip, half], theirs_b, sums_b, landed_b, kept_b, reached_b,
        swap_send_b, swap_recv_b, plane_send_b, plane_recv_b, row_send_b, row_recv_b,
    )


def on_device(sizes, scenes, cotangent, params, partials):
    scenes, cotangent = scenes[0], cotangent[0]
    height, width, channels = scenes.shape
    n = sizes[0] * sizes[1] * sizes[2] // 2
    rows = params.size // LANES
    dma = pltpu.SemaphoreType.DMA
    half_type, full = jnp.bfloat16, jnp.float32
    anywhere, vmem = pl.BlockSpec(memory_space=pl.ANY), pl.BlockSpec(memory_space=pltpu.VMEM)
    cat = pltpu.VMEM((height + 2, width, 3 * channels), half_type)
    tall = pltpu.VMEM((9 * channels, channels), half_type)
    acc = pltpu.VMEM((channels, 9 * channels), full)
    lines, m = sizes[1], n // sizes[1]
    chunks = [
        pltpu.VMEM((n, rows, LANES), full),
        pltpu.VMEM((n - lines, rows, LANES), half_type),
        pltpu.VMEM((lines, m - 1, rows, LANES), half_type),
        pltpu.VMEM((lines, rows, LANES), full),
        pltpu.VMEM((lines - 1, rows, LANES), full),
    ]
    sum_sems = [dma, dma((n,)), dma, dma((lines,)), dma, dma]
    scratch = [
        pltpu.VMEM(scenes.shape, half_type),
        pltpu.VMEM(scenes.shape, half_type),
        pltpu.VMEM((4, 2, width, channels), half_type),
        pltpu.VMEM((len(AROUND), 2, width, channels), half_type),
        cat,
        cat,
        pltpu.VMEM((2, height, channels), full),
        pltpu.VMEM((18 * channels, channels), full),
        tall,
        tall,
        acc,
        acc,
        pltpu.VMEM((n, 2, rows, LANES), half_type),
        pltpu.VMEM((n, 2, rows, LANES), full),
        pltpu.VMEM((n, rows, LANES), full),
        pltpu.VMEM((1, 1, LANES), full),
        pltpu.VMEM((2 * n - 1, 1, LANES), full),
        pltpu.VMEM((rows, LANES), half_type),
        *chunks,
        *chunks,
        dma((2,)), dma((n,)),
        dma, dma, dma, dma((lines - 1,)), dma((n - lines,)), dma, dma, dma, dma,
        *sum_sems,
        *sum_sems,
    ]
    grads = pl.pallas_call(
        functools.partial(kernel, sizes, 16),
        out_shape=jax.ShapeDtypeStruct((rows, LANES), full),
        in_specs=[anywhere, vmem, anywhere, anywhere],
        out_specs=vmem,
        scratch_shapes=scratch,
        compiler_params=pltpu.CompilerParams(
            collective_id=0, has_side_effects=True, vmem_limit_bytes=56 * 2**20
        ),
        name="sam_grad",
    )(partials[0].reshape(n, 2, rows, LANES), params.reshape(rows, LANES), scenes, cotangent)
    return grads.reshape(-1)


def solution(mesh):
    sizes = tuple(mesh.shape[axis] for axis in AXES)
    return jax.shard_map(
        functools.partial(on_device, sizes),
        mesh=mesh,
        in_specs=(
            P("scene", "row", "col", None),
            P("scene", "row", "col", None),
            P(AXES),
            P(AXES, None),
        ),
        out_specs=P(AXES),
        check_vma=False,
    )
```
